32 devices in a mesh: rows: 4 (over x, core), cols: 8 (over z, y).
Axes of the slice: x: 2, y: 2, z: 4, core: 2. Of those that a mesh axis runs over, the one named last changes fastest.
Arguments:
- image: bfloat16 [48, 64, 2048], P(None, 'rows', 'cols'), may hold values from -6 to 6
- perturb: float32 [48, 64, 2048], P(None, 'rows', 'cols'), may hold values from -0.5 to 0.5
- target: bfloat16 [48, 32, 1024], P(None, 'rows', 'cols'), may hold values from -6 to 6
- kernel_one: float32 [48, 48, 3, 3], replicated, may hold values from -0.3125 to 0.3125
- kernel_two: float32 [48, 48, 3, 3], replicated, may hold values from -0.3125 to 0.3125
- moment_one: float32 [48, 48, 3, 3], replicated, may hold values from -6 to 6
- moment_two: float32 [48, 48, 3, 3], replicated, may hold values from -6 to 6
Outputs:
- new_perturb: float32 [48, 64, 2048], P(None, 'rows', 'cols')
- prediction: bfloat16 [48, 32, 1024], P(None, 'rows', 'cols')
- new_kernel_one: float32 [48, 48, 3, 3], replicated
- new_kernel_two: float32 [48, 48, 3, 3], replicated
- new_moment_one: float32 [48, 48, 3, 3], replicated
- new_moment_two: float32 [48, 48, 3, 3], replicated
The draws below stay inside these ranges and needn't reach their ends.
All inputs are finite; a program needn't handle non-finite values.
Results may differ from the reference program's by a relative error of at most 0.0085.
Values may be sent and summed in bfloat16 or wider, within the bound.
A program may use at most 128 MiB of HBM per device.

```python
import jax
import jax.numpy as jnp
from jax import lax

C = 48
REPLAYS = 3
HEIGHT = 64
WIDTH = 2048


def steps_of(key, shape, cuts, smallest, largest):
    def one(dim, parts):
        heights = jax.random.uniform(jax.random.fold_in(jax.random.fold_in(key, 6), dim), (parts,), jnp.float32, smallest / len(cuts), largest / len(cuts))
        return jnp.repeat(jnp.exp(heights), shape[dim] // parts).reshape((-1,) + (1,) * (len(shape) - dim - 1))

    factor_of = one(*cuts[0])
    for cut in cuts[1:]:
        factor_of = factor_of * one(*cut)
    return factor_of


def normal_values(key, shape, width, most, cuts=(), dtype=jnp.bfloat16):
    result = width * jax.random.normal(key, shape, jnp.float32)
    if cuts:
        result = result * steps_of(key, shape, cuts, -0.22, 0.18)
    return jnp.clip(result, -most, most).astype(dtype)


def setup_inputs(seed: int = 0) -> dict:
    seeds = jax.random.split(jax.random.key(seed), 8)
    return {
        "image": normal_values(seeds[0], (C, HEIGHT, WIDTH), 1.0, 6.0, ((1, 4), (2, 8))),
        "perturb": jnp.clip(jax.random.uniform(seeds[1], (C, HEIGHT, WIDTH), jnp.float32, -0.5, 0.5) * steps_of(seeds[1], (C, HEIGHT, WIDTH), ((1, 4), (2, 8)), -0.4, 0.0), -0.5, 0.5),
        "target": normal_values(seeds[2], (C, HEIGHT // 2, WIDTH // 2), 1.0, 6.0, ((1, 4), (2, 8))),
        "kernel_one": normal_values(seeds[3], (C, C, 3, 3), (9 * C) ** -0.5, 0.3125, (), jnp.float32),
        "kernel_two": normal_values(seeds[4], (C, C, 3, 3), (9 * C) ** -0.5, 0.3125, (), jnp.float32),
        "moment_one": normal_values(seeds[5], (C, C, 3, 3), 1.0, 6.0, (), jnp.float32),
        "moment_two": normal_values(seeds[6], (C, C, 3, 3), 1.0, 6.0, (), jnp.float32),
    }


step_size = 0.5
clip_bound = 0.5
momentum_rate = 0.9
learn_rate = 0.005
mean_epsilon = 1e-06
numbers = ('NCHW', 'OIHW', 'NCHW')

def rounded(values):
    return lax.optimization_barrier(values.astype(jnp.bfloat16)).astype(jnp.float32)

def dilated_conv(source, kernel):
    return lax.conv_general_dilated(source[None], kernel, (1, 1), ((2, 2), (2, 2)), rhs_dilation=(2, 2), dimension_numbers=numbers, precision=lax.Precision.HIGHEST)[0]

def strided_conv(source, kernel):
    return lax.conv_general_dilated(source[None], kernel, (2, 2), ((1, 1), (1, 1)), dimension_numbers=numbers, precision=lax.Precision.HIGHEST)[0]

def silu_slope(pre_value):
    sigmoid_value = jax.nn.sigmoid(pre_value)
    return sigmoid_value * (1.0 + pre_value * (1.0 - sigmoid_value))

def normed_update(kernel, moment, gradient):
    moment = momentum_rate * moment + gradient / jnp.sqrt(jnp.mean(gradient * gradient) + mean_epsilon)
    return (kernel - learn_rate * moment, moment)

def reference(image, perturb, target, kernel_one, kernel_two, moment_one, moment_two):
    target_wide = target.astype(jnp.float32)
    predict = jnp.zeros(target.shape, jnp.float32)
    for replay in range(REPLAYS):
        fast_one = rounded(kernel_one)
        fast_two = rounded(kernel_two)
        attacked = rounded(image.astype(jnp.float32) + perturb)
        hidden_pre, pull_one = jax.vjp(dilated_conv, attacked, fast_one)
        hidden = rounded(jax.nn.silu(hidden_pre))
        predict, pull_two = jax.vjp(strided_conv, hidden, fast_two)
        residual = rounded(predict - target_wide)
        hidden_grad, grad_two = pull_two(residual)
        pre_grad = rounded(hidden_grad * silu_slope(hidden_pre))
        input_grad, grad_one = pull_one(pre_grad)
        perturb = jnp.clip(perturb + step_size * jnp.tanh(input_grad), -clip_bound, clip_bound)
        kernel_one, moment_one = normed_update(kernel_one, moment_one, grad_one)
        kernel_two, moment_two = normed_update(kernel_two, moment_two, grad_two)
    return (perturb, predict.astype(jnp.bfloat16), kernel_one, kernel_two, moment_one, moment_two)
```

```python
import functools

import jax
import jax.numpy as jnp
import ml_dtypes
import numpy as np
from jax import lax
from jax.experimental import pallas as pl
from jax.experimental.pallas import tpu as pltpu
from jax.sharding import PartitionSpec as P

REPLAYS = 3

step_size = 0.5
clip_bound = 0.5
momentum_rate = 0.9
learn_rate = 0.005
mean_epsilon = 1e-06

MESH = pl.DeviceIdType.MESH
BF16 = jnp.bfloat16
F32 = jnp.float32
RIM = 3
LANES = 128
VMEM_LIMIT = 56 * 1024 * 1024
WHOLE = pl.BlockSpec(memory_space=pltpu.VMEM)

SIDES = ((0, -1), (0, 1), (-1, -1), (-1, 1), (1, -1), (1, 1))
TAPS = [(a, b) for a in range(3) for b in range(3)]


class Flat:
    def __init__(self, channels, rows, cols):
        self.channels, self.rows, self.cols = channels, rows, cols
        self.pitch = cols + 16
        self.total = -(-((rows + 2 * RIM) * self.pitch) // LANES) * LANES
        self.lift = rows * self.pitch
        self.edge = -(-(RIM * self.pitch) // LANES) * LANES
        first = RIM * self.pitch
        self.own_low = first // LANES * LANES
        self.own_high = -(-(first + self.lift) // LANES) * LANES
        self.down_from = self.own_low
        self.band = self.total - (self.down_from + self.lift)
        self.half = -(-9 * channels // (2 * LANES)) * LANES
        assert self.lift % LANES == 0 and self.edge <= self.band
        groups = self.places()
        self.families = []
        for members in ((0,), (1,), (2, 3), (4, 5)):
            low = groups[members[0]][1]
            width = sum(len(groups[j][2]) for j in members)
            assert 4 * width <= LANES
            self.families.append((members, low, width))

    def at(self, row, col):
        return (row + RIM) * self.pitch + col + RIM

    def places(self):
        groups = []
        lane = 0
        for down, right in SIDES:
            rows = {0: range(self.rows), -1: range(self.rows - RIM, self.rows), 1: range(RIM)}[down]
            cols = {-1: range(self.cols - RIM, self.cols), 1: range(RIM)}[right]
            pairs = [(r, c) for r in rows for c in cols]
            groups.append(((down, right), lane, pairs))
            lane += len(pairs)
        assert lane <= LANES
        return groups

    def tables(self):
        pack = np.zeros((self.total, LANES), ml_dtypes.bfloat16)
        unpack = np.zeros((LANES, self.total), ml_dtypes.bfloat16)
        for (down, right), lane, pairs in self.places():
            for k, (r, c) in enumerate(pairs):
                pack[self.at(r, c), lane + k] = 1
                unpack[lane + k, self.at(r + down * self.rows, c + right * self.cols)] = 1
        spots = np.arange(self.total)
        where = np.zeros((8, self.total), np.int32)
        where[0] = spots // self.pitch - RIM
        where[1] = spots % self.pitch - RIM
        return pack, unpack, where


def dot(a, b):
    return jnp.dot(a, b, preferred_element_type=F32)


def dot_nt(a, b):
    return lax.dot_general(a, b, (((1,), (1,)), ((), ())), preferred_element_type=F32)


def dot_exact(values, table):
    high = values.astype(BF16)
    rest = values - high.astype(F32)
    middle = rest.astype(BF16)
    low = (rest - middle.astype(F32)).astype(BF16)
    return dot(high, table) + (dot(middle, table) + dot(low, table))


def rolled(values, shift):
    if shift % values.shape[1] == 0:
        return values
    return pltpu.roll(values, (-shift) % values.shape[1], axis=1)


def whole_kernel(flat, row_count, col_count, *refs):
    (image_in, perturb_in, target_in, k1_in, k2_in, m1_in, m2_in, pack, unpack, where) = refs[:10]
    (perturb_out, predict_out, k1_out, k2_out, m1_out, m2_out) = refs[10:16]
    (
        ext, attacked_cols, slope, hidden, hidden_cols, rest_cols, pre_cols,
        own, target_own, image, perturb, target,
        message, target_message, above, below, beside, target_above, target_below, target_beside,
        state, moment, weights, back_wide, spread_wide, spread_weight,
        grad, grad_sent, grad_mate, plane, line, summed,
        rim_sends, rim_recvs, sum_sends, sum_recvs, rows_wide, rows_short,
    ) = refs[16:]
    C, N, T, H = flat.channels, flat.total, flat.pitch, flat.half
    K = 9 * C
    w = flat.cols
    low, high = flat.own_low, flat.own_high
    me_row, me_col = lax.axis_index("rows"), lax.axis_index("cols")
    core, chip = lax.rem(me_row, 2), me_row // 2
    near, far = lax.rem(me_col, 2), me_col // 2
    chips, lines = row_count // 2, col_count // 2
    me_plane = chip * 2 + near
    last = REPLAYS - 1

    def exists(down, right):
        return (
            (me_row + down >= 0)
            & (me_row + down < row_count)
            & (me_col + right >= 0)
            & (me_col + right < col_count)
        )

    mate = {"rows": me_row + 1 - 2 * core, "cols": me_col}
    plane_peers = []
    for dx in range(chips):
        for dy in range(2):
            if dx or dy:
                there = lax.rem(chip + dx, chips) * 2 + core
                plane_peers.append({"rows": there, "cols": far * 2 + lax.rem(near + dy, 2)})
    line_peers = [
        {"rows": me_row, "cols": lax.rem(far + d, lines) * 2 + near} for d in range(1, lines)
    ]

    barrier = pltpu.get_barrier_semaphore()

    def signal(device):
        pl.semaphore_signal(barrier, inc=1, device_id=device, device_id_type=MESH)

    greeted = 1 + len(plane_peers) + len(line_peers)
    signal(mate)
    for device in plane_peers + line_peers:
        signal(device)
    for down, right in SIDES + ((1, 0), (-1, 0)):
        there = exists(down, right)
        pl.when(there)(
            functools.partial(signal, {"rows": me_row + down, "cols": me_col + right})
        )
        greeted = greeted + there.astype(jnp.int32)

    lane = lax.broadcasted_iota(jnp.int32, (1, LANES), 1)

    from_col = lax.broadcasted_iota(jnp.int32, (2 * w, 2 * w), 0)
    to_col = lax.broadcasted_iota(jnp.int32, (2 * w, 2 * w), 1)
    sorted_from = jnp.where(to_col < w, 2 * to_col, 2 * (to_col - w) + 1)
    order = (from_col == sorted_from).astype(F32).astype(BF16)
    high_rows = 2 * flat.rows

    def apart(parts):
        rows_wide[0] = parts[:, :w]
        rows_wide[1] = parts[:, w:]

    own[...] = jnp.zeros(own.shape, BF16)
    ext[...] = jnp.zeros(ext.shape, F32)
    perturb[...] = jnp.zeros(perturb.shape, F32)
    hidden[...] = jnp.zeros(hidden.shape, F32)

    apart(dot(image_in[...], order))
    for r in range(flat.rows):
        spot = flat.at(r, 0)
        for py in range(2):
            for px in range(2):
                part = rows_wide[px, pl.ds(2 * r + py, C, stride=high_rows), :]
                hidden[2 * py + px, :, spot : spot + w] = part
    apart(dot_exact(perturb_in[...], order))
    for r in range(flat.rows):
        spot = flat.at(r, 0)
        for py in range(2):
            for px in range(2):
                part = rows_wide[px, pl.ds(2 * r + py, C, stride=high_rows), :]
                perturb[2 * py + px, :, spot : spot + w] = part
    rows_short[...] = target_in[...].astype(F32)
    for r in range(flat.rows):
        spot = flat.at(r, 0)
        ext[:, spot : spot + w] = rows_short[pl.ds(r, C, stride=flat.rows), :]
    target_own[0] = ext[...].astype(BF16)

    def make_message(k):
        phases = [dot(own[k, p, :, low:high], pack[low:high, :]) for p in range(4)]
        for f, (_, first, width) in enumerate(flat.families):
            tile = jnp.zeros((C, LANES), F32)
            for p in range(4):
                keep = (lane >= p * width) & (lane < (p + 1) * width)
                tile = jnp.where(keep, rolled(phases[p], first - p * width), tile)
            message[k, f] = tile.astype(BF16)

    target_message[...] = dot(target_own[0], pack[...]).astype(BF16)
    for p in range(4):
        image[p] = hidden[p].astype(BF16)
        own[0, p] = (hidden[p] + perturb[p]).astype(BF16)
    make_message(0)
    pl.semaphore_wait(barrier, greeted)

    def copy_of(source, target, sends, recvs, device):
        return pltpu.make_async_remote_copy(
            src_ref=source,
            dst_ref=target,
            send_sem=sends,
            recv_sem=recvs,
            device_id=device,
            device_id_type=MESH,
        )

    family_of = {j: f for f, (members, _, _) in enumerate(flat.families) for j in members}

    def rim_copies(from_own, sides, to_above, to_below, to_beside, k):
        copies = []

        def add(source, target, down, right):
            i = len(copies)
            device = {"rows": me_row + down, "cols": me_col + right}
            copy = copy_of(source, target, rim_sends.at[k, i], rim_recvs.at[k, i], device)
            copies.append((copy, exists(down, right), exists(-down, -right)))

        one, two = flat.lift, flat.lift + flat.edge
        add(from_own.at[:, :, one:two], to_above, 1, 0)
        one, two = flat.down_from, flat.down_from + flat.band
        add(from_own.at[:, :, one:two], to_below, -1, 0)
        for j, (down, right) in enumerate(SIDES):
            add(sides(j), to_beside.at[j], -down, -right)
        return copies

    def start(copies):
        for copy, there, _ in copies:
            pl.when(there)(copy.start)

    def finish(copies):
        for copy, there, here in copies:
            pl.when(there)(copy.wait_send)
            pl.when(here)(copy.wait_recv)

    def rim_of(k):
        return rim_copies(
            own.at[k],
            lambda j: message.at[k, family_of[j]],
            above.at[k],
            below.at[k],
            beside.at[k],
            k,
        )

    begin = rim_of(0)
    start(begin)
    extra = rim_copies(
        target_own, lambda j: target_message, target_above, target_below, target_beside, REPLAYS
    )
    start(extra)

    row, col = where[0:1, :], where[1:2, :]
    owned = ((row >= 0) & (row < flat.rows) & (col >= 0) & (col < flat.cols)).astype(F32)
    owned = owned[:, low:high]
    far_row, far_col = row + me_row * flat.rows, col + me_col * flat.cols
    inside = (
        (far_row >= 0)
        & (far_row < flat.rows * row_count)
        & (far_col >= 0)
        & (far_col < flat.cols * col_count)
    ).astype(F32)
    has_above, has_below = me_row > 0, me_row < row_count - 1
    end = flat.down_from + flat.lift

    state[...] = jnp.zeros(state.shape, F32)
    moment[...] = jnp.zeros(moment.shape, F32)
    grad[...] = jnp.zeros(grad.shape, F32)
    weights[...] = jnp.zeros(weights.shape, F32)
    back_wide[...] = jnp.zeros(back_wide.shape, F32)
    spread_wide[...] = jnp.zeros(spread_wide.shape, F32)
    for i in range(9):
        one, two = i * C, (i + 1) * C
        state[0, :, one:two] = k1_in[one:two, :]
        state[1, :, one:two] = k2_in[one:two, :]
        moment[0, :, one:two] = m1_in[one:two, :]
        moment[1, :, one:two] = m2_in[one:two, :]

    groups = flat.places()

    def extend(block, gathered, top, bottom):
        ext[...] = block.astype(F32) + dot(gathered.astype(BF16), unpack[...])
        ext[:, 0 : flat.edge] += jnp.where(has_above, top.astype(F32), 0.0)
        ext[:, end:N] += jnp.where(has_below, bottom.astype(F32), 0.0)

    def attacked_ready(k):
        parts = []
        for members, _, width in flat.families:
            part = jnp.zeros((C, LANES), F32)
            each = width // len(members)
            for m, j in enumerate(members):
                (down, right), _, _ = groups[j]
                inner = lax.rem(lane, width)
                keep = (inner >= m * each) & (inner < (m + 1) * each) & exists(down, right)
                part = jnp.where(keep, beside[k, j].astype(F32), part)
            parts.append(part)
        for p in range(4):
            gathered = jnp.zeros((C, LANES), F32)
            for f, (_, first, width) in enumerate(flat.families):
                keep = (lane >= first) & (lane < first + width)
                gathered = jnp.where(keep, rolled(parts[f], p * width - first), gathered)
            extend(own[k, p], gathered, above[k, p], below[k, p])
            full = ext[...].astype(BF16)
            for i, (a, b) in enumerate(TAPS):
                attacked_cols[p, i * C : (i + 1) * C, :] = rolled(full, (a - 1) * T + (b - 1))

    finish(begin)
    finish(extra)
    gathered = jnp.zeros((C, LANES), F32)
    for j, ((down, right), first, pairs) in enumerate(groups):
        keep = (lane >= first) & (lane < first + len(pairs)) & exists(down, right)
        gathered = jnp.where(keep, target_beside[j].astype(F32), gathered)
    extend(target_own[0], gathered, target_above[0], target_below[0])
    target[...] = ext[...]
    attacked_ready(0)

    def mate_copy(k, g):
        return copy_of(
            grad_sent.at[k, g, 1 - core],
            grad_mate.at[k, g],
            sum_sends.at[k, g, 0],
            sum_recvs.at[k, g, 0],
            mate,
        )

    def peer_copies(ref, index, peers, k, g, at):
        return [
            copy_of(
                ref.at[k, g, index],
                ref.at[k, g, index],
                sum_sends.at[k, g, at + i],
                sum_recvs.at[k, g, at + i],
                device,
            )
            for i, device in enumerate(peers)
        ]

    def plane_copies(k, g):
        return peer_copies(plane, me_plane, plane_peers, k, g, 2)

    def line_copies(k, g):
        return peer_copies(line, far, line_peers, k, g, 2 + len(plane_peers))

    def back_copies(k, g):
        return peer_copies(summed, core, [mate], k, g, 1)

    def begin_sum(k, g, total):
        grad[g, 0] = total[:, :H]
        grad[g, 1, :, 0 : K - H] = total[:, H:]
        grad_sent[k, g] = grad[g].astype(BF16)
        mate_copy(k, g).start()

    def plane_sum(k, g):
        mate_copy(k, g).wait()
        plane[k, g, me_plane] = (grad[g, core] + grad_mate[k, g].astype(F32)).astype(BF16)
        for copy in plane_copies(k, g):
            copy.start()

    def sum_of(ref, k, g, count):
        total = ref[k, g, 0].astype(F32)
        for i in range(1, count):
            total = total + ref[k, g, i].astype(F32)
        return total.astype(BF16)

    def line_sum(k, g):
        for copy in plane_copies(k, g):
            copy.wait()
        line[k, g, far] = sum_of(plane, k, g, 2 * chips)
        for copy in line_copies(k, g):
            copy.start()

    def back_sum(k, g):
        for copy in line_copies(k, g):
            copy.wait()
        summed[k, g, core] = sum_of(line, k, g, lines)
        for copy in back_copies(k, g):
            copy.start()

    def end_sum(k, g):
        for copy in back_copies(k, g):
            copy.wait()
        parts = [summed[k, g, h].astype(F32) for h in range(2)]
        squares = parts[0] * parts[0] + parts[1] * parts[1]
        mean = jnp.sum(jnp.sum(squares, axis=0, keepdims=True), axis=1, keepdims=True) / (K * C)
        scale = jnp.sqrt(mean + mean_epsilon)
        for h in range(2):
            later = momentum_rate * moment[g, :, h * H : (h + 1) * H] + parts[h] / scale
            moment[g, :, h * H : (h + 1) * H] = later
            state[g, :, h * H : (h + 1) * H] -= learn_rate * later

    def replay(k):
        fast_one, fast_two = state[0, :, 0:K].astype(BF16), state[1, :, 0:K].astype(BF16)
        for g in range(2):
            weights[g * C : (g + 1) * C, :] = state[g]
        turned = jnp.transpose(weights[...])
        for i, (a, b) in enumerate(TAPS):
            py, dy = [(1, 1), (0, 0), (1, 0)][a]
            px, dx = [(1, 1), (0, 0), (1, 0)][b]
            block = turned[i * C : (i + 1) * C, :]
            back_wide[:, i * C : (i + 1) * C] = block[:, 0:C]
            p, slot = 2 * py + px, 2 * dy + dx
            spread_wide[p * C : (p + 1) * C, slot * C : (slot + 1) * C] = block[:, C : 2 * C]
        spread_weight[...] = spread_wide[:, 0 : 4 * C].astype(BF16)

        for p in range(4):
            pre_value = dot(fast_one, attacked_cols[p])
            sigmoid_value = jax.nn.sigmoid(pre_value)
            hidden[p] = pre_value * sigmoid_value * inside
            slope[p] = sigmoid_value * (1.0 + pre_value * (1.0 - sigmoid_value)) * inside
        for i, (a, b) in enumerate(TAPS):
            py, dy = [(1, -1), (0, 0), (1, 0)][a]
            px, dx = [(1, -1), (0, 0), (1, 0)][b]
            moved = rolled(hidden[2 * py + px].astype(BF16), dy * T + dx)
            hidden_cols[i * C : (i + 1) * C, :] = moved
        predict = dot(fast_two, hidden_cols[...])
        ext[...] = predict
        residual = ((predict - target[...]) * inside).astype(BF16)
        mine = (residual[:, low:high].astype(F32) * owned).astype(BF16)
        begin_sum(k, 1, dot_nt(mine, hidden_cols[:, low:high]))
        for i, shift in enumerate((0, 1, T, T + 1)):
            rest_cols[i * C : (i + 1) * C, :] = rolled(residual, shift)
        hidden_grad = dot(spread_weight[...], rest_cols[...])
        total = jnp.zeros((C, K), F32)
        for p in range(4):
            pre_grad = hidden_grad[p * C : (p + 1) * C, :] * slope[p]
            hidden[p] = pre_grad
            mine = (pre_grad[:, low:high] * owned).astype(BF16)
            total = total + dot_nt(mine, attacked_cols[p, :, low:high])
        plane_sum(k, 1)
        begin_sum(k, 0, total)

        back_one = back_wide[:, 0:K].astype(BF16)

        def input_side(p):
            pre_grad = hidden[p].astype(BF16)
            for i, (a, b) in enumerate(TAPS):
                moved = rolled(pre_grad, -((a - 1) * T + (b - 1)))
                pre_cols[i * C : (i + 1) * C, :] = moved[:, low:high]
            input_grad = dot(back_one, pre_cols[...])
            moved = jnp.clip(
                perturb[p, :, low:high] + step_size * jnp.tanh(input_grad), -clip_bound, clip_bound
            )
            moved = moved * owned
            perturb[p, :, low:high] = moved
            own[k + 1, p, :, low:high] = (image[p, :, low:high].astype(F32) + moved).astype(BF16)

        input_side(0)
        plane_sum(k, 0)
        for p in range(1, 4):
            input_side(p)
        following = rim_of(k + 1)

        @pl.when(k < last)
        def _():
            make_message(k + 1)
            start(following)

        line_sum(k, 1)
        line_sum(k, 0)

        @pl.when(k < last)
        def _():
            finish(following)
            attacked_ready(k + 1)

        @pl.when(k == last)
        def _():
            for r in range(flat.rows):
                spot = flat.at(r, 0)
                rows_short[pl.ds(r, C, stride=flat.rows), :] = ext[:, spot : spot + w]
                for py in range(2):
                    for px in range(2):
                        part = perturb[2 * py + px, :, spot : spot + w]
                        rows_wide[px, pl.ds(2 * r + py, C, stride=high_rows), :] = part
            predict_out[...] = rows_short[...].astype(BF16)
            back_order = (
                lax.broadcasted_iota(jnp.int32, (2 * w, 2 * w), 1)
                == jnp.where(from_col < w, 2 * from_col, 2 * (from_col - w) + 1)
            ).astype(F32).astype(BF16)
            perturb_out[...] = dot_exact(rows_wide[0], back_order[:w, :]) + dot_exact(
                rows_wide[1], back_order[w:, :]
            )

        for g in (1, 0):
            back_sum(k, g)
        for g in (1, 0):
            end_sum(k, g)

    @pl.loop(0, REPLAYS)
    def _(k):
        replay(k)

    for i in range(9):
        one, two = i * C, (i + 1) * C
        k1_out[one:two, :] = state[0, :, one:two]
        k2_out[one:two, :] = state[1, :, one:two]
        m1_out[one:two, :] = moment[0, :, one:two]
        m2_out[one:two, :] = moment[1, :, one:two]


def whole(flat, operands):
    C, N, H = flat.channels, flat.total, flat.half
    K = 9 * C
    row_count, col_count = lax.axis_size("rows"), lax.axis_size("cols")
    assert row_count % 2 == 0 and col_count % 2 == 0
    width = flat.own_high - flat.own_low
    image, perturb, target = operands[:3]
    shapes = [
        jax.ShapeDtypeStruct(perturb.shape, F32),
        jax.ShapeDtypeStruct(target.shape, BF16),
    ] + [jax.ShapeDtypeStruct((K, C), F32)] * 4
    sums = 2 + (row_count - 1) + (col_count // 2 - 1)
    scratch = [
        pltpu.VMEM((C, N), F32),
        pltpu.VMEM((4, K, N), BF16),
        pltpu.VMEM((4, C, N), F32),
        pltpu.VMEM((4, C, N), F32),
        pltpu.VMEM((K, N), BF16),
        pltpu.VMEM((4 * C, N), BF16),
        pltpu.VMEM((K, width), BF16),
        pltpu.VMEM((REPLAYS + 1, 4, C, N), BF16),
        pltpu.VMEM((1, C, N), BF16),
        pltpu.VMEM((4, C, N), BF16),
        pltpu.VMEM((4, C, N), F32),
        pltpu.VMEM((C, N), F32),
        pltpu.VMEM((REPLAYS, 4, C, LANES), BF16),
        pltpu.VMEM((C, LANES), BF16),
        pltpu.VMEM((REPLAYS, 4, C, flat.edge), BF16),
        pltpu.VMEM((REPLAYS, 4, C, flat.band), BF16),
        pltpu.VMEM((REPLAYS, len(SIDES), C, LANES), BF16),
        pltpu.VMEM((1, C, flat.edge), BF16),
        pltpu.VMEM((1, C, flat.band), BF16),
        pltpu.VMEM((len(SIDES), C, LANES), BF16),
        pltpu.VMEM((2, C, 2 * H), F32),
        pltpu.VMEM((2, C, 2 * H), F32),
        pltpu.VMEM((LANES, 2 * H), F32),
        pltpu.VMEM((C, 2 * H), F32),
        pltpu.VMEM((4 * C, 2 * LANES), F32),
        pltpu.VMEM((4 * C, 4 * C), BF16),
        pltpu.VMEM((2, 2, C, H), F32),
        pltpu.VMEM((REPLAYS, 2, 2, C, H), BF16),
        pltpu.VMEM((REPLAYS, 2, C, H), BF16),
        pltpu.VMEM((REPLAYS, 2, row_count, C, H), BF16),
        pltpu.VMEM((REPLAYS, 2, col_count // 2, C, H), BF16),
        pltpu.VMEM((REPLAYS, 2, 2, C, H), BF16),
        pltpu.SemaphoreType.DMA((REPLAYS + 1, 8)),
        pltpu.SemaphoreType.DMA((REPLAYS + 1, 8)),
        pltpu.SemaphoreType.DMA((REPLAYS, 2, sums)),
        pltpu.SemaphoreType.DMA((REPLAYS, 2, sums)),
        pltpu.VMEM((2, perturb.shape[0], flat.cols), F32),
        pltpu.VMEM(target.shape, F32),
    ]
    return pl.pallas_call(
        functools.partial(whole_kernel, flat, row_count, col_count),
        out_shape=shapes,
        in_specs=[WHOLE] * len(operands),
        out_specs=[WHOLE] * len(shapes),
        scratch_shapes=scratch,
        compiler_params=pltpu.CompilerParams(
            collective_id=0, has_side_effects=True, vmem_limit_bytes=VMEM_LIMIT
        ),
    )(*operands)


def body(image, perturb, target, *kernels):
    C = image.shape[0]
    flat = Flat(C, target.shape[1], target.shape[2])
    tables = [jnp.asarray(t) for t in flat.tables()]
    merged = [x.reshape(-1, x.shape[2]) for x in (image, perturb, target)]
    kernels = [x.transpose(2, 3, 0, 1).reshape(9 * C, C) for x in kernels]
    new_perturb, prediction, *kernels = whole(flat, merged + kernels + tables)
    kernels = [x.reshape(3, 3, C, C).transpose(2, 3, 0, 1) for x in kernels]
    return (new_perturb.reshape(perturb.shape), prediction.reshape(target.shape), *kernels)


def solution(mesh):
    block = P(None, "rows", "cols")
    in_specs = (block, block, block, P(), P(), P(), P())
    out_specs = (block, block, P(), P(), P(), P())
    return jax.shard_map(body, mesh=mesh, in_specs=in_specs, out_specs=out_specs, check_vma=False)
```

```python
import functools

import jax
import jax.numpy as jnp
import ml_dtypes
import numpy as np
from jax import lax
from jax.experimental import pallas as pl
from jax.experimental.pallas import tpu as pltpu
from jax.sharding import PartitionSpec as P

REPLAYS = 3

step_size = 0.5
clip_bound = 0.5
momentum_rate = 0.9
learn_rate = 0.005
mean_epsilon = 1e-06

MESH = pl.DeviceIdType.MESH
BF16 = jnp.bfloat16
F32 = jnp.float32
RIM = 3
LANES = 128
VMEM_LIMIT = 56 * 1024 * 1024
WHOLE = pl.BlockSpec(memory_space=pltpu.VMEM)

SIDES = ((0, -1), (0, 1), (-1, -1), (-1, 1), (1, -1), (1, 1))
TAPS = [(a, b) for a in range(3) for b in range(3)]


SIDE_COLS = (-3, -2, -1, 0)
PITCH = 9


class Tiles:
    def __init__(self, channels, rows, cols):
        self.channels, self.rows, self.cols = channels, rows, cols
        self.tall = rows + 2 * RIM
        self.total = (self.tall + 1) * LANES
        self.half = -(-9 * channels // (2 * LANES)) * LANES
        assert cols == LANES and self.tall * PITCH <= LANES
        groups = self.places()
        self.families = []
        for members in ((0,), (1,), (2, 3), (4, 5)):
            low = groups[members[0]][1]
            width = sum(len(groups[j][2]) for j in members)
            assert 4 * width <= LANES
            self.families.append((members, low, width))

    def side(self, row, col):
        return (row + RIM) * PITCH + (col + RIM if col <= 0 else col - self.cols + 6)

    def places(self):
        groups = []
        lane = 0
        for down, right in SIDES:
            rows = {0: range(self.rows), -1: range(self.rows - RIM, self.rows), 1: range(RIM)}[down]
            cols = {-1: range(self.cols - RIM, self.cols), 1: range(RIM)}[right]
            pairs = [(r, c) for r in rows for c in cols]
            groups.append(((down, right), lane, pairs))
            lane += len(pairs)
        assert lane <= LANES
        return groups

    def tables(self):
        kind = ml_dtypes.bfloat16
        pack = np.zeros((self.rows * LANES, LANES), kind)
        settle = np.zeros((LANES, LANES), kind)
        for (down, right), lane, pairs in self.places():
            for k, (r, c) in enumerate(pairs):
                pack[r * LANES + c, lane + k] = 1
                settle[lane + k, self.side(r + down * self.rows, c + right * self.cols)] = 1
        place = np.zeros((4, LANES, 4 * LANES), kind)
        unplace = np.zeros((4 * LANES, 4 * LANES), kind)
        for f, (_, low, width) in enumerate(self.families):
            for p in range(4):
                for i in range(width):
                    spot = f * LANES + p * width + i
                    place[p, low + i, spot] = 1
                    unplace[spot, p * LANES : (p + 1) * LANES] = settle[low + i]
        pick = np.zeros((self.tall * LANES, LANES), kind)
        where = np.zeros((8, self.total), np.int32)
        where[0, :] = -(10**6)
        for t in range(self.tall):
            where[0, t * LANES : (t + 1) * LANES] = t - RIM
            where[1, t * LANES : (t + 1) * LANES] = np.arange(LANES)
            for col in (0, self.cols - 2, self.cols - 1):
                pick[t * LANES + col, self.side(t - RIM, col)] = 1
            for col in SIDE_COLS + tuple(range(self.cols - 2, self.cols + RIM)):
                spot = self.tall * LANES + self.side(t - RIM, col)
                where[0, spot], where[1, spot] = t - RIM, col
        return pack, place, unplace, settle, pick, where


def dot(a, b):
    return jnp.dot(a, b, preferred_element_type=F32)


def dot_nt(a, b):
    return lax.dot_general(a, b, (((1,), (1,)), ((), ())), preferred_element_type=F32)


def dot_exact(values, table):
    high = values.astype(BF16)
    rest = values - high.astype(F32)
    middle = rest.astype(BF16)
    low = (rest - middle.astype(F32)).astype(BF16)
    return dot(high, table) + (dot(middle, table) + dot(low, table))


def rolled(values, shift):
    if shift % values.shape[1] == 0:
        return values
    return pltpu.roll(values, (-shift) % values.shape[1], axis=1)


def whole_kernel(tiles, row_count, col_count, *refs):
    sources = refs[:13]
    (perturb_out, predict_out, k1_out, k2_out, m1_out, m2_out) = refs[13:19]
    held = refs[19:32]
    (image_in, perturb_in, target_in, pack, place, unplace, settle, pick, where) = held[:9]
    (k1_in, k2_in, m1_in, m2_in) = held[9:]
    (
        attacked, attacked_three, slope, hidden, hidden_three, rest, pre, pre_stack, pre_three,
        image, perturb, target_main, target, predicted,
        message, target_message, beside, target_beside,
        state, moment, weights, back_wide, spread_wide, spread_weight,
        grad_wide, grad, grad_sent, grad_mate, plane, line, summed,
        load_sems, rim_sends, rim_recvs, sum_sends, sum_recvs, rows_wide, rows_short,
    ) = refs[32:]
    C, H, L, tall = tiles.channels, tiles.half, LANES, tiles.tall
    K, C3 = 9 * C, 3 * C
    rows, w = tiles.rows, tiles.cols
    own = slice(RIM * L, (RIM + rows) * L)
    me_row, me_col = lax.axis_index("rows"), lax.axis_index("cols")
    core, chip = lax.rem(me_row, 2), me_row // 2
    near, far = lax.rem(me_col, 2), me_col // 2
    chips, lines = row_count // 2, col_count // 2
    me_plane = chip * 2 + near
    last = REPLAYS - 1

    def exists(down, right):
        return (
            (me_row + down >= 0)
            & (me_row + down < row_count)
            & (me_col + right >= 0)
            & (me_col + right < col_count)
        )

    mate = {"rows": me_row + 1 - 2 * core, "cols": me_col}
    plane_peers = []
    for dx in range(chips):
        for dy in range(2):
            if dx or dy:
                there = lax.rem(chip + dx, chips) * 2 + core
                plane_peers.append({"rows": there, "cols": far * 2 + lax.rem(near + dy, 2)})
    line_peers = [
        {"rows": me_row, "cols": lax.rem(far + d, lines) * 2 + near} for d in range(1, lines)
    ]

    barrier = pltpu.get_barrier_semaphore()

    def signal(device):
        pl.semaphore_signal(barrier, inc=1, device_id=device, device_id_type=MESH)

    greeted = 1 + len(plane_peers) + len(line_peers)
    for device in line_peers + plane_peers + [mate]:
        signal(device)
    for down, right in SIDES + ((1, 0), (-1, 0)):
        there = exists(down, right)
        pl.when(there)(
            functools.partial(signal, {"rows": me_row + down, "cols": me_col + right})
        )
        greeted = greeted + there.astype(jnp.int32)

    loads = [
        pltpu.make_async_copy(source, target, load_sems.at[i])
        for i, (source, target) in enumerate(zip(sources, held))
    ]
    for load in loads:
        load.start()

    lane = lax.broadcasted_iota(jnp.int32, (1, L), 1)

    @pl.when(me_row == 0)
    def _():
        for k in range(REPLAYS):
            attacked[k, :, :, 0 : RIM * L] = jnp.zeros((4, C, RIM * L), BF16)
        target_main[0, :, 0 : RIM * L] = jnp.zeros((C, RIM * L), BF16)

    @pl.when(me_row == row_count - 1)
    def _():
        for k in range(REPLAYS):
            attacked[k, :, :, (RIM + rows) * L :] = jnp.zeros((4, C, RIM * L), BF16)
        target_main[0, :, (RIM + rows) * L :] = jnp.zeros((C, RIM * L), BF16)

    from_col = lax.broadcasted_iota(jnp.int32, (2 * w, 2 * w), 0)
    to_col = lax.broadcasted_iota(jnp.int32, (2 * w, 2 * w), 1)
    sorted_from = jnp.where(to_col < w, 2 * to_col, 2 * (to_col - w) + 1)
    order = (from_col == sorted_from).astype(F32).astype(BF16)
    high_rows = 2 * rows

    def spread_rows(parts, put):
        rows_wide[0] = parts[:, :w]
        rows_wide[1] = parts[:, w:]
        for r in range(rows):
            for py in range(2):
                for px in range(2):
                    part = rows_wide[px, pl.ds(2 * r + py, C, stride=high_rows), :]
                    put(2 * py + px, slice(r * L, (r + 1) * L), part)

    def put_image(p, spots, part):
        image[p, :, spots] = part.astype(BF16)

    def put_perturb(p, spots, part):
        perturb[p, :, spots] = part

    loads[0].wait()
    spread_rows(dot(image_in[...], order), put_image)
    loads[1].wait()
    spread_rows(dot_exact(perturb_in[...], order), put_perturb)
    for p in range(4):
        attacked[0, p, :, own] = (image[p].astype(F32) + perturb[p]).astype(BF16)
    loads[2].wait()
    rows_short[...] = target_in[...].astype(F32)
    for r in range(rows):
        spot = (RIM + r) * L
        target_main[0, :, spot : spot + L] = rows_short[pl.ds(r, C, stride=rows), :].astype(BF16)

    def make_message(k):
        phases = [dot(attacked[k, p, :, own], pack[...]).astype(BF16) for p in range(4)]
        total = dot(phases[0], place[0])
        for p in range(1, 4):
            total = total + dot(phases[p], place[p])
        for f in range(4):
            message[k, f] = total[:, f * L : (f + 1) * L].astype(BF16)

    loads[3].wait()
    loads[4].wait()
    make_message(0)
    target_message[...] = dot(target_main[0, :, own], pack[...]).astype(BF16)
    pl.semaphore_wait(barrier, greeted)

    def copy_of(source, target, sends, recvs, device):
        return pltpu.make_async_remote_copy(
            src_ref=source,
            dst_ref=target,
            send_sem=sends,
            recv_sem=recvs,
            device_id=device,
            device_id_type=MESH,
        )

    family_of = {j: f for f, (members, _, _) in enumerate(tiles.families) for j in members}

    def rim_copies(block, sides, to_beside, k):
        copies = []

        def add(source, target, down, right):
            i = len(copies)
            device = {"rows": me_row + down, "cols": me_col + right}
            copy = copy_of(source, target, rim_sends.at[k, i], rim_recvs.at[k, i], device)
            copies.append((copy, exists(down, right), exists(-down, -right)))

        for j, (down, right) in enumerate(SIDES):
            add(sides(j), to_beside.at[j], -down, -right)
        deep = RIM * L
        add(block.at[:, :, pl.ds(rows * L, deep)], block.at[:, :, pl.ds(0, deep)], 1, 0)
        add(block.at[:, :, pl.ds(deep, deep)], block.at[:, :, pl.ds(deep + rows * L, deep)], -1, 0)
        return copies

    def start(copies):
        for copy, there, _ in copies:
            pl.when(there)(copy.start)

    def finish(copies):
        for copy, there, here in copies:
            pl.when(there)(copy.wait_send)
            pl.when(here)(copy.wait_recv)

    def rim_of(k):
        return rim_copies(attacked.at[k], lambda j: message.at[k, family_of[j]], beside.at[k], k)

    begin = rim_of(0)
    start(begin)
    extra = rim_copies(target_main, lambda j: target_message, target_beside, REPLAYS)
    start(extra)

    for load in loads[5:]:
        load.wait()
    far_row, far_col = where[0:1, :] + me_row * rows, where[1:2, :] + me_col * w
    inside = (
        (far_row >= 0)
        & (far_row < rows * row_count)
        & (far_col >= 0)
        & (far_col < w * col_count)
    ).astype(F32)
    inside_side = inside[:, tall * L :]
    tall_one, tall_two, tall_three = rows + 4, rows + 3, rows + 2
    inside_one = jnp.concatenate([inside[:, L : (1 + tall_one) * L], inside_side], axis=1)
    inside_two = jnp.concatenate([inside[:, 2 * L : (2 + tall_two) * L], inside_side], axis=1)

    state[...] = jnp.zeros(state.shape, F32)
    moment[...] = jnp.zeros(moment.shape, F32)
    grad_wide[...] = jnp.zeros(grad_wide.shape, F32)
    weights[...] = jnp.zeros(weights.shape, F32)
    spread_wide[...] = jnp.zeros(spread_wide.shape, F32)
    pre_stack[...] = jnp.zeros(pre_stack.shape, BF16)
    for i in range(9):
        one, two = i * C, (i + 1) * C
        state[0, :, one:two] = k1_in[one:two, :]
        state[1, :, one:two] = k2_in[one:two, :]
        moment[0, :, one:two] = m1_in[one:two, :]
        moment[1, :, one:two] = m2_in[one:two, :]

    groups = tiles.places()
    slot_of = lax.rem(lane, PITCH)

    def shifted(block, edge, by):
        end = 0 if by < 0 else L - 1
        return jnp.where(lane == end, edge, pltpu.roll(block, (-by) % L, axis=1))

    def edges(side):
        return jnp.where(slot_of == 2, side, pltpu.roll(side, L - 5, axis=1))

    def edge(both, row):
        return pltpu.roll(both, (-tiles.side(row, -1)) % L, axis=1)

    def attacked_ready(k):
        parts = []
        for members, _, width in tiles.families:
            part = jnp.zeros((C, L), F32)
            each = width // len(members)
            for m, j in enumerate(members):
                (down, right), _, _ = groups[j]
                inner = lax.rem(lane, width)
                keep = (inner >= m * each) & (inner < (m + 1) * each) & exists(down, right)
                part = jnp.where(keep, beside[k, j].astype(F32), part)
            parts.append(jnp.where(lane < 4 * width, part, 0.0).astype(BF16))
        around = dot(jnp.concatenate(parts, axis=1), unplace[...])
        for p in range(4):
            side = around[:, p * L : (p + 1) * L] + dot(attacked[k, p], pick[...])
            both = edges(side)
            for t in range(tall):
                spots = slice(t * L, (t + 1) * L)
                block = attacked[k, p, :, spots].astype(F32)
                ends = edge(both, t - RIM)
                attacked_three[p, 0:C, spots] = shifted(block, ends, -1).astype(BF16)
                attacked_three[p, C : 2 * C, spots] = attacked[k, p, :, spots]
                attacked_three[p, 2 * C :, spots] = shifted(block, ends, 1).astype(BF16)
            spots = slice(tall * L, (tall + 1) * L)
            attacked_three[p, 0:C, spots] = pltpu.roll(side, 1, axis=1).astype(BF16)
            attacked_three[p, C : 2 * C, spots] = side.astype(BF16)
            attacked_three[p, 2 * C :, spots] = pltpu.roll(side, L - 1, axis=1).astype(BF16)

    finish(begin)
    attacked_ready(0)
    finish(extra)
    gathered = jnp.zeros((C, L), F32)
    for j, ((down, right), first, pairs) in enumerate(groups):
        keep = (lane >= first) & (lane < first + len(pairs)) & exists(down, right)
        gathered = jnp.where(keep, target_beside[j].astype(F32), gathered)
    target[:, 0 : tall_two * L] = target_main[0, :, 2 * L : (2 + tall_two) * L].astype(F32)
    target[:, tall_two * L :] = dot(gathered.astype(BF16), settle[...]) + dot(
        target_main[0], pick[...]
    )

    def mate_copy(k, g):
        return copy_of(
            grad_sent.at[k, g, 1 - core],
            grad_mate.at[k, g],
            sum_sends.at[k, g, 0],
            sum_recvs.at[k, g, 0],
            mate,
        )

    def peer_copies(ref, index, peers, k, g, at):
        return [
            copy_of(
                ref.at[k, g, index],
                ref.at[k, g, index],
                sum_sends.at[k, g, at + i],
                sum_recvs.at[k, g, at + i],
                device,
            )
            for i, device in enumerate(peers)
        ]

    def plane_copies(k, g):
        return peer_copies(plane, me_plane, plane_peers, k, g, 2)

    def line_copies(k, g):
        return peer_copies(line, far, line_peers, k, g, 2 + len(plane_peers))

    def back_copies(k, g):
        return peer_copies(summed, core, [mate], k, g, 1)

    def begin_sum(k, g, parts):
        for a in range(3):
            grad_wide[g, :, a * C3 : (a + 1) * C3] = parts[a]
        for h in range(2):
            grad[g, h] = grad_wide[g, :, h * H : (h + 1) * H]
            grad_sent[k, g, h] = grad_wide[g, :, h * H : (h + 1) * H].astype(BF16)
        mate_copy(k, g).start()

    def plane_sum(k, g):
        mate_copy(k, g).wait()
        plane[k, g, me_plane] = (grad[g, core] + grad_mate[k, g].astype(F32)).astype(BF16)
        for copy in plane_copies(k, g):
            copy.start()

    def sum_of(ref, k, g, count):
        total = ref[k, g, 0].astype(F32)
        for i in range(1, count):
            total = total + ref[k, g, i].astype(F32)
        return total.astype(BF16)

    def line_sum(k, g):
        for copy in plane_copies(k, g):
            copy.wait()
        line[k, g, far] = sum_of(plane, k, g, 2 * chips)
        for copy in line_copies(k, g):
            copy.start()

    def back_sum(k, g):
        for copy in line_copies(k, g):
            copy.wait()
        summed[k, g, core] = sum_of(line, k, g, lines)
        for copy in back_copies(k, g):
            copy.start()

    def end_sum(k, g):
        for copy in back_copies(k, g):
            copy.wait()
        parts = [summed[k, g, h].astype(F32) for h in range(2)]
        squares = parts[0] * parts[0] + parts[1] * parts[1]
        mean = jnp.sum(jnp.sum(squares, axis=0, keepdims=True), axis=1, keepdims=True) / (K * C)
        scale = jnp.sqrt(mean + mean_epsilon)
        for h in range(2):
            later = momentum_rate * moment[g, :, h * H : (h + 1) * H] + parts[h] / scale
            moment[g, :, h * H : (h + 1) * H] = later
            state[g, :, h * H : (h + 1) * H] -= learn_rate * later

    def replay(k):
        fast_one = [state[0, :, a * C3 : (a + 1) * C3].astype(BF16) for a in range(3)]
        fast_two = [state[1, :, a * C3 : (a + 1) * C3].astype(BF16) for a in range(3)]
        ahead_one = jnp.concatenate(fast_one, axis=0)
        for g in range(2):
            weights[g * C : (g + 1) * C, :] = state[g]
        turned = jnp.transpose(weights[...])
        for i, (a, b) in enumerate(TAPS):
            py, dy = [(1, 1), (0, 0), (1, 0)][a]
            px, dx = [(1, 1), (0, 0), (1, 0)][b]
            block = turned[i * C : (i + 1) * C, :]
            back_wide[a * C : (a + 1) * C, b * C : (b + 1) * C] = block[:, 0:C]
            p, slot = 2 * py + px, 2 * dy + dx
            spread_wide[p * C : (p + 1) * C, slot * C : (slot + 1) * C] = block[:, C : 2 * C]
        spread_weight[...] = spread_wide[:, 0 : 4 * C].astype(BF16)

        for p in (1, 3, 0, 2):
            sums = dot(ahead_one, attacked_three[p])
            main = (
                sums[0:C, 0 : tall_one * L]
                + sums[C : 2 * C, L : (1 + tall_one) * L]
                + sums[2 * C :, 2 * L : (2 + tall_one) * L]
            )
            side = sums[:, tall * L :]
            side = (
                pltpu.roll(side[0:C], PITCH, axis=1)
                + side[C : 2 * C]
                + pltpu.roll(side[2 * C :], L - PITCH, axis=1)
            )
            pre_value = jnp.concatenate([main, side], axis=1)
            sigmoid_value = jax.nn.sigmoid(pre_value)
            value = pre_value * sigmoid_value * inside_one
            slope_value = sigmoid_value * (1.0 + pre_value * (1.0 - sigmoid_value)) * inside_one
            slope[p, :, 0 : tall_three * L] = slope_value[:, L : (1 + tall_three) * L]
            slope[p, :, tall_three * L :] = slope_value[:, tall_one * L :]
            py, px = p // 2, p % 2
            if px == 0:
                hidden_three[py, C : 2 * C, :] = value.astype(BF16)
            else:
                hidden_three[py, 2 * C :, :] = value.astype(BF16)
                side = value[:, tall_one * L :]
                for t in range(tall_one):
                    spots = slice(t * L, (t + 1) * L)
                    moved = shifted(value[:, spots], edge(side, t - 2), -1)
                    hidden_three[py, 0:C, spots] = moved.astype(BF16)
                hidden_three[py, 0:C, tall_one * L :] = pltpu.roll(side, 1, axis=1).astype(BF16)

        outer = dot(jnp.concatenate([fast_two[0], fast_two[2]], axis=0), hidden_three[1])
        middle = dot(fast_two[1], hidden_three[0])
        main = (
            outer[0:C, 0 : tall_two * L]
            + outer[C:, L : (1 + tall_two) * L]
            + middle[:, L : (1 + tall_two) * L]
        )
        side = (
            pltpu.roll(outer[0:C, tall_one * L :], PITCH, axis=1)
            + outer[C:, tall_one * L :]
            + middle[:, tall_one * L :]
        )
        predicted[...] = main[:, L : (1 + rows) * L]
        predict = jnp.concatenate([main, side], axis=1)
        residual = ((predict - target[...]) * inside_two).astype(BF16)
        mine = residual[:, L : (1 + rows) * L]
        begin_sum(
            k,
            1,
            [
                dot_nt(mine, hidden_three[1, :, L : (1 + rows) * L]),
                dot_nt(mine, hidden_three[0, :, 2 * L : (2 + rows) * L]),
                dot_nt(mine, hidden_three[1, :, 2 * L : (2 + rows) * L]),
            ],
        )

        wide = residual.astype(F32)
        side = wide[:, tall_two * L :]
        for t in range(tall_two):
            spot = tiles.side(t - 1, 0)
            first = pltpu.roll(wide[:, t * L : (t + 1) * L], spot, axis=1)
            side = jnp.where(lane == spot, first, side)
        moved = []
        for t in range(tall_two):
            ends = pltpu.roll(side, (L - 1 - tiles.side(t - 1, w)) % L, axis=1)
            moved.append(shifted(wide[:, t * L : (t + 1) * L], ends, 1))
        moved = jnp.concatenate(moved, axis=1)
        moved_side = pltpu.roll(side, L - 1, axis=1)
        for i, (dy, block, beyond) in enumerate(
            ((0, wide, side), (0, moved, moved_side), (1, wide, side), (1, moved, moved_side))
        ):
            part = slice(i * C, (i + 1) * C)
            rest[part, 0 : tall_three * L] = block[:, dy * L : (dy + tall_three) * L].astype(BF16)
            beyond = rolled(beyond, dy * PITCH)
            rest[part, tall_three * L :] = beyond.astype(BF16)
        hidden_grad = dot(spread_weight[...], rest[...])
        total = jnp.zeros((C3, C3), F32)
        for p in range(4):
            pre_grad = (hidden_grad[p * C : (p + 1) * C, :] * slope[p]).astype(BF16)
            pre[p] = pre_grad
            for a in range(3):
                part = slice(a * C, (a + 1) * C)
                pre_stack[p, part, a * L : (a + rows) * L] = pre_grad[:, L : (1 + rows) * L]
            total = total + dot_nt(pre_stack[p], attacked_three[p, :, 2 * L : (2 + tall_three) * L])
        plane_sum(k, 1)
        begin_sum(k, 0, [total[a * C : (a + 1) * C, :] for a in range(3)])

        back_one = back_wide[:, 0:C3].astype(BF16)

        def input_side(p):
            side = pre[p, :, tall_three * L :].astype(F32)
            both = edges(side)
            for t in range(tall_three):
                spots = slice(t * L, (t + 1) * L)
                block = pre[p, :, spots].astype(F32)
                ends = edge(both, t - 1)
                pre_three[0:C, spots] = shifted(block, ends, 1).astype(BF16)
                pre_three[C : 2 * C, spots] = pre[p, :, spots]
                pre_three[2 * C :, spots] = shifted(block, ends, -1).astype(BF16)
            sums = dot(back_one, pre_three[...])
            input_grad = (
                sums[0:C, 2 * L : (2 + rows) * L]
                + sums[C : 2 * C, L : (1 + rows) * L]
                + sums[2 * C :, 0 : rows * L]
            )
            moved = jnp.clip(perturb[p] + step_size * jnp.tanh(input_grad), -clip_bound, clip_bound)
            perturb[p] = moved
            attacked[k + 1, p, :, own] = (image[p].astype(F32) + moved).astype(BF16)

        input_side(0)
        plane_sum(k, 0)
        for p in range(1, 4):
            input_side(p)
        following = rim_of(k + 1)

        @pl.when(k < last)
        def _():
            make_message(k + 1)
            start(following)

        line_sum(k, 1)
        line_sum(k, 0)

        @pl.when(k < last)
        def _():
            finish(following)
            attacked_ready(k + 1)

        @pl.when(k == last)
        def _():
            for r in range(rows):
                spots = slice(r * L, (r + 1) * L)
                rows_short[pl.ds(r, C, stride=rows), :] = predicted[:, spots]
                for py in range(2):
                    for px in range(2):
                        part = perturb[2 * py + px, :, spots]
                        rows_wide[px, pl.ds(2 * r + py, C, stride=high_rows), :] = part
            predict_out[...] = rows_short[...].astype(BF16)
            back_order = (
                lax.broadcasted_iota(jnp.int32, (2 * w, 2 * w), 1)
                == jnp.where(from_col < w, 2 * from_col, 2 * (from_col - w) + 1)
            ).astype(F32).astype(BF16)
            perturb_out[...] = dot_exact(rows_wide[0], back_order[:w, :]) + dot_exact(
                rows_wide[1], back_order[w:, :]
            )

        for g in (1, 0):
            back_sum(k, g)
        for g in (1, 0):
            end_sum(k, g)

    @pl.loop(0, REPLAYS)
    def _(k):
        replay(k)

    for i in range(9):
        one, two = i * C, (i + 1) * C
        k1_out[one:two, :] = state[0, :, one:two]
        k2_out[one:two, :] = state[1, :, one:two]
        m1_out[one:two, :] = moment[0, :, one:two]
        m2_out[one:two, :] = moment[1, :, one:two]


def whole(tiles, operands):
    C, H, L = tiles.channels, tiles.half, LANES
    K, C3, rows = 9 * C, 3 * C, tiles.rows
    row_count, col_count = lax.axis_size("rows"), lax.axis_size("cols")
    assert row_count % 2 == 0 and col_count % 2 == 0
    perturb, target = operands[1:3]
    shapes = [
        jax.ShapeDtypeStruct(perturb.shape, F32),
        jax.ShapeDtypeStruct(target.shape, BF16),
    ] + [jax.ShapeDtypeStruct((K, C), F32)] * 4
    sums = 2 + (row_count - 1) + (col_count // 2 - 1)
    scratch = [pltpu.VMEM(x.shape, x.dtype) for x in operands] + [
        pltpu.VMEM((REPLAYS + 1, 4, C, tiles.tall * L), BF16),
        pltpu.VMEM((4, C3, tiles.total), BF16),
        pltpu.VMEM((4, C, (rows + 3) * L), F32),
        pltpu.VMEM((8, L), F32),
        pltpu.VMEM((2, C3, (rows + 5) * L), BF16),
        pltpu.VMEM((4 * C, (rows + 3) * L), BF16),
        pltpu.VMEM((4, C, (rows + 3) * L), BF16),
        pltpu.VMEM((4, C3, (rows + 2) * L), BF16),
        pltpu.VMEM((C3, (rows + 2) * L), BF16),
        pltpu.VMEM((4, C, rows * L), BF16),
        pltpu.VMEM((4, C, rows * L), F32),
        pltpu.VMEM((1, C, tiles.tall * L), BF16),
        pltpu.VMEM((C, (rows + 4) * L), F32),
        pltpu.VMEM((C, rows * L), F32),
        pltpu.VMEM((REPLAYS, 4, C, L), BF16),
        pltpu.VMEM((C, L), BF16),
        pltpu.VMEM((REPLAYS, len(SIDES), C, L), BF16),
        pltpu.VMEM((len(SIDES), C, L), BF16),
        pltpu.VMEM((2, C, 2 * H), F32),
        pltpu.VMEM((2, C, 2 * H), F32),
        pltpu.VMEM((L, 2 * H), F32),
        pltpu.VMEM((C3, 2 * L), F32),
        pltpu.VMEM((4 * C, 2 * L), F32),
        pltpu.VMEM((4 * C, 4 * C), BF16),
        pltpu.VMEM((2, C, 2 * H), F32),
        pltpu.VMEM((2, 2, C, H), F32),
        pltpu.VMEM((REPLAYS, 2, 2, C, H), BF16),
        pltpu.VMEM((REPLAYS, 2, C, H), BF16),
        pltpu.VMEM((REPLAYS, 2, row_count, C, H), BF16),
        pltpu.VMEM((REPLAYS, 2, col_count // 2, C, H), BF16),
        pltpu.VMEM((REPLAYS, 2, 2, C, H), BF16),
        pltpu.SemaphoreType.DMA((len(operands),)),
        pltpu.SemaphoreType.DMA((REPLAYS + 1, 8)),
        pltpu.SemaphoreType.DMA((REPLAYS + 1, 8)),
        pltpu.SemaphoreType.DMA((REPLAYS, 2, sums)),
        pltpu.SemaphoreType.DMA((REPLAYS, 2, sums)),
        pltpu.VMEM((2, perturb.shape[0], L), F32),
        pltpu.VMEM(target.shape, F32),
    ]
    return pl.pallas_call(
        functools.partial(whole_kernel, tiles, row_count, col_count),
        out_shape=shapes,
        in_specs=[pl.BlockSpec(memory_space=pl.ANY)] * len(operands),
        out_specs=[WHOLE] * len(shapes),
        scratch_shapes=scratch,
        compiler_params=pltpu.CompilerParams(
            collective_id=0, has_side_effects=True, vmem_limit_bytes=VMEM_LIMIT
        ),
    )(*operands)


def body(image, perturb, target, *kernels):
    C = image.shape[0]
    tiles = Tiles(C, target.shape[1], target.shape[2])
    tables = [jnp.asarray(t) for t in tiles.tables()]
    merged = [x.reshape(-1, x.shape[2]) for x in (image, perturb, target)]
    kernels = [x.transpose(2, 3, 0, 1).reshape(9 * C, C) for x in kernels]
    new_perturb, prediction, *kernels = whole(tiles, merged + tables + kernels)
    kernels = [x.reshape(3, 3, C, C).transpose(2, 3, 0, 1) for x in kernels]
    return (new_perturb.reshape(perturb.shape), prediction.reshape(target.shape), *kernels)


def solution(mesh):
    block = P(None, "rows", "cols")
    in_specs = (block, block, block, P(), P(), P(), P())
    out_specs = (block, block, P(), P(), P(), P())
    return jax.shard_map(body, mesh=mesh, in_specs=in_specs, out_specs=out_specs, check_vma=False)
```

```python
import functools

import jax
import jax.numpy as jnp
import ml_dtypes
import numpy as np
from jax import lax
from jax.experimental import pallas as pl
from jax.experimental.pallas import tpu as pltpu
from jax.sharding import PartitionSpec as P

REPLAYS = 3

step_size = 0.5
clip_bound = 0.5
momentum_rate = 0.9
learn_rate = 0.005
mean_epsilon = 1e-06

MESH = pl.DeviceIdType.MESH
BF16 = jnp.bfloat16
F32 = jnp.float32
RIM = 3
LANES = 128
VMEM_LIMIT = 56 * 1024 * 1024
FINISH_LIMIT = 16 * 1024 * 1024
WHOLE = pl.BlockSpec(memory_space=pltpu.VMEM)

SIDES = ((0, -1), (0, 1), (-1, -1), (-1, 1), (1, -1), (1, 1))
TAPS = [(a, b) for a in range(3) for b in range(3)]


SIDE_COLS = (-3, -2, -1, 0)
PITCH = 9


class Tiles:
    def __init__(self, channels, rows, cols):
        self.channels, self.rows, self.cols = channels, rows, cols
        self.tall = rows + 2 * RIM
        self.total = (self.tall + 1) * LANES
        self.half = -(-9 * channels // (2 * LANES)) * LANES
        assert cols == LANES and self.tall * PITCH <= LANES
        groups = self.places()
        self.families = []
        for members in ((0,), (1,), (2, 3), (4, 5)):
            low = groups[members[0]][1]
            width = sum(len(groups[j][2]) for j in members)
            assert 4 * width <= LANES
            self.families.append((members, low, width))

    def side(self, row, col):
        return (row + RIM) * PITCH + (col + RIM if col <= 0 else col - self.cols + 6)

    def places(self):
        groups = []
        lane = 0
        for down, right in SIDES:
            rows = {0: range(self.rows), -1: range(self.rows - RIM, self.rows), 1: range(RIM)}[down]
            cols = {-1: range(self.cols - RIM, self.cols), 1: range(RIM)}[right]
            pairs = [(r, c) for r in rows for c in cols]
            groups.append(((down, right), lane, pairs))
            lane += len(pairs)
        assert lane <= LANES
        return groups

    def tables(self):
        kind = ml_dtypes.bfloat16
        pack = np.zeros((self.rows * LANES, LANES), kind)
        settle = np.zeros((LANES, LANES), kind)
        for (down, right), lane, pairs in self.places():
            for k, (r, c) in enumerate(pairs):
                pack[r * LANES + c, lane + k] = 1
                settle[lane + k, self.side(r + down * self.rows, c + right * self.cols)] = 1
        place = np.zeros((4, LANES, 4 * LANES), kind)
        unplace = np.zeros((4 * LANES, 4 * LANES), kind)
        for f, (_, low, width) in enumerate(self.families):
            for p in range(4):
                for i in range(width):
                    spot = f * LANES + p * width + i
                    place[p, low + i, spot] = 1
                    unplace[spot, p * LANES : (p + 1) * LANES] = settle[low + i]
        pick = np.zeros((self.tall * LANES, LANES), kind)
        where = np.zeros((8, self.total), np.int32)
        where[0, :] = -(10**6)
        for t in range(self.tall):
            where[0, t * LANES : (t + 1) * LANES] = t - RIM
            where[1, t * LANES : (t + 1) * LANES] = np.arange(LANES)
            for col in (0, self.cols - 2, self.cols - 1):
                pick[t * LANES + col, self.side(t - RIM, col)] = 1
            for col in SIDE_COLS + tuple(range(self.cols - 2, self.cols + RIM)):
                spot = self.tall * LANES + self.side(t - RIM, col)
                where[0, spot], where[1, spot] = t - RIM, col
        return pack, place, unplace, settle, pick, where


def dot(a, b):
    return jnp.dot(a, b, preferred_element_type=F32)


def dot_nt(a, b):
    return lax.dot_general(a, b, (((1,), (1,)), ((), ())), preferred_element_type=F32)


def dot_exact(values, table):
    high = values.astype(BF16)
    rest = values - high.astype(F32)
    middle = rest.astype(BF16)
    low = (rest - middle.astype(F32)).astype(BF16)
    return dot(high, table) + (dot(middle, table) + dot(low, table))


def rolled(values, shift):
    if shift % values.shape[1] == 0:
        return values
    return pltpu.roll(values, (-shift) % values.shape[1], axis=1)


def whole_kernel(tiles, row_count, col_count, *refs):
    sources = refs[:13]
    (perturb_rows, predict_rows, state, moment) = refs[13:17]
    held = refs[17:30]
    (image_in, perturb_in, target_in, pack, place, unplace, settle, pick, where) = held[:9]
    (k1_in, k2_in, m1_in, m2_in) = held[9:]
    (
        attacked, attacked_three, slope, hidden_three, rest, pre, pre_stack, pre_three,
        image, perturb, target_main, target, predicted,
        message, target_message, beside, target_beside,
        weights, back_wide, spread_wide, spread_weight,
        grad_wide, grad, grad_sent, grad_mate, plane, line, summed,
        load_sems, rim_sends, rim_recvs, sum_sends, sum_recvs, rows_wide, rows_short,
    ) = refs[30:]
    C, H, L, tall = tiles.channels, tiles.half, LANES, tiles.tall
    K, C3 = 9 * C, 3 * C
    rows, w = tiles.rows, tiles.cols
    own = slice(RIM * L, (RIM + rows) * L)
    me_row, me_col = lax.axis_index("rows"), lax.axis_index("cols")
    core, chip = lax.rem(me_row, 2), me_row // 2
    near, far = lax.rem(me_col, 2), me_col // 2
    chips, lines = row_count // 2, col_count // 2
    me_plane = chip * 2 + near
    last = REPLAYS - 1

    def exists(down, right):
        return (
            (me_row + down >= 0)
            & (me_row + down < row_count)
            & (me_col + right >= 0)
            & (me_col + right < col_count)
        )

    mate = {"rows": me_row + 1 - 2 * core, "cols": me_col}
    plane_peers = []
    for dx in range(chips):
        for dy in range(2):
            if dx or dy:
                there = lax.rem(chip + dx, chips) * 2 + core
                plane_peers.append({"rows": there, "cols": far * 2 + lax.rem(near + dy, 2)})
    line_peers = [
        {"rows": me_row, "cols": lax.rem(far + d, lines) * 2 + near} for d in range(1, lines)
    ]

    barrier = pltpu.get_barrier_semaphore()

    def signal(device):
        pl.semaphore_signal(barrier, inc=1, device_id=device, device_id_type=MESH)

    greeted = 1 + len(plane_peers) + len(line_peers)
    for device in line_peers + plane_peers + [mate]:
        signal(device)
    for down, right in SIDES + ((1, 0), (-1, 0)):
        there = exists(down, right)
        pl.when(there)(
            functools.partial(signal, {"rows": me_row + down, "cols": me_col + right})
        )
        greeted = greeted + there.astype(jnp.int32)

    loads = [
        pltpu.make_async_copy(source, target, load_sems.at[i])
        for i, (source, target) in enumerate(zip(sources, held))
    ]
    for load in loads:
        load.start()

    lane = lax.broadcasted_iota(jnp.int32, (1, L), 1)

    @pl.when(me_row == 0)
    def _():
        for k in range(REPLAYS):
            attacked[k, :, :, 0 : RIM * L] = jnp.zeros((4, C, RIM * L), BF16)
        target_main[0, :, 0 : RIM * L] = jnp.zeros((C, RIM * L), BF16)

    @pl.when(me_row == row_count - 1)
    def _():
        for k in range(REPLAYS):
            attacked[k, :, :, (RIM + rows) * L :] = jnp.zeros((4, C, RIM * L), BF16)
        target_main[0, :, (RIM + rows) * L :] = jnp.zeros((C, RIM * L), BF16)

    from_col = lax.broadcasted_iota(jnp.int32, (2 * w, 2 * w), 0)
    to_col = lax.broadcasted_iota(jnp.int32, (2 * w, 2 * w), 1)
    sorted_from = jnp.where(to_col < w, 2 * to_col, 2 * (to_col - w) + 1)
    order = (from_col == sorted_from).astype(F32).astype(BF16)
    high_rows = 2 * rows

    def spread_rows(parts, put):
        rows_wide[0] = parts[:, :w]
        rows_wide[1] = parts[:, w:]
        for r in range(rows):
            for py in range(2):
                for px in range(2):
                    part = rows_wide[px, pl.ds(2 * r + py, C, stride=high_rows), :]
                    put(2 * py + px, slice(r * L, (r + 1) * L), part)

    def put_image(p, spots, part):
        image[p, :, spots] = part.astype(BF16)

    def put_perturb(p, spots, part):
        perturb[p, :, spots] = part

    loads[0].wait()
    spread_rows(dot(image_in[...], order), put_image)
    loads[1].wait()
    spread_rows(dot_exact(perturb_in[...], order), put_perturb)
    for p in range(4):
        attacked[0, p, :, own] = (image[p].astype(F32) + perturb[p]).astype(BF16)
    loads[2].wait()
    rows_short[...] = target_in[...].astype(F32)
    for r in range(rows):
        spot = (RIM + r) * L
        target_main[0, :, spot : spot + L] = rows_short[pl.ds(r, C, stride=rows), :].astype(BF16)

    def make_message(k):
        phases = [dot(attacked[k, p, :, own], pack[...]).astype(BF16) for p in range(4)]
        total = dot(phases[0], place[0])
        for p in range(1, 4):
            total = total + dot(phases[p], place[p])
        for f in range(4):
            message[k, f] = total[:, f * L : (f + 1) * L].astype(BF16)

    loads[3].wait()
    loads[4].wait()
    make_message(0)
    target_message[...] = dot(target_main[0, :, own], pack[...]).astype(BF16)
    pl.semaphore_wait(barrier, greeted)

    def copy_of(source, target, sends, recvs, device):
        return pltpu.make_async_remote_copy(
            src_ref=source,
            dst_ref=target,
            send_sem=sends,
            recv_sem=recvs,
            device_id=device,
            device_id_type=MESH,
        )

    family_of = {j: f for f, (members, _, _) in enumerate(tiles.families) for j in members}

    def rim_copies(block, sides, to_beside, k):
        copies = []

        def add(source, target, down, right):
            i = len(copies)
            device = {"rows": me_row + down, "cols": me_col + right}
            copy = copy_of(source, target, rim_sends.at[k, i], rim_recvs.at[k, i], device)
            copies.append((copy, exists(down, right), exists(-down, -right)))

        for j, (down, right) in enumerate(SIDES):
            add(sides(j), to_beside.at[j], -down, -right)
        deep = RIM * L
        add(block.at[:, :, pl.ds(rows * L, deep)], block.at[:, :, pl.ds(0, deep)], 1, 0)
        add(block.at[:, :, pl.ds(deep, deep)], block.at[:, :, pl.ds(deep + rows * L, deep)], -1, 0)
        return copies

    def start(copies):
        for copy, there, _ in copies:
            pl.when(there)(copy.start)

    def finish(copies):
        for copy, there, here in copies:
            pl.when(there)(copy.wait_send)
            pl.when(here)(copy.wait_recv)

    def rim_of(k):
        return rim_copies(attacked.at[k], lambda j: message.at[k, family_of[j]], beside.at[k], k)

    begin = rim_of(0)
    start(begin)
    extra = rim_copies(target_main, lambda j: target_message, target_beside, REPLAYS)
    start(extra)

    for load in loads[5:]:
        load.wait()
    far_row, far_col = where[0:1, :] + me_row * rows, where[1:2, :] + me_col * w
    inside = (
        (far_row >= 0)
        & (far_row < rows * row_count)
        & (far_col >= 0)
        & (far_col < w * col_count)
    ).astype(F32)
    inside_side = inside[:, tall * L :]
    tall_one, tall_two, tall_three = rows + 4, rows + 3, rows + 2
    inside_one = jnp.concatenate([inside[:, L : (1 + tall_one) * L], inside_side], axis=1)
    inside_two = jnp.concatenate([inside[:, 2 * L : (2 + tall_two) * L], inside_side], axis=1)

    state[...] = jnp.zeros(state.shape, F32)
    moment[...] = jnp.zeros(moment.shape, F32)
    grad_wide[...] = jnp.zeros(grad_wide.shape, F32)
    weights[...] = jnp.zeros(weights.shape, F32)
    spread_wide[...] = jnp.zeros(spread_wide.shape, F32)
    pre_stack[...] = jnp.zeros(pre_stack.shape, BF16)
    for i in range(9):
        one, two = i * C, (i + 1) * C
        state[0, :, one:two] = k1_in[one:two, :]
        state[1, :, one:two] = k2_in[one:two, :]
        moment[0, :, one:two] = m1_in[one:two, :]
        moment[1, :, one:two] = m2_in[one:two, :]

    groups = tiles.places()
    slot_of = lax.rem(lane, PITCH)

    def shifted(block, edge, by):
        end = 0 if by < 0 else L - 1
        return jnp.where(lane == end, edge, pltpu.roll(block, (-by) % L, axis=1))

    def edges(side):
        return jnp.where(slot_of == 2, side, pltpu.roll(side, L - 5, axis=1))

    def edge(both, row):
        return pltpu.roll(both, (-tiles.side(row, -1)) % L, axis=1)

    def attacked_ready(k):
        parts = []
        for members, _, width in tiles.families:
            part = jnp.zeros((C, L), F32)
            each = width // len(members)
            for m, j in enumerate(members):
                (down, right), _, _ = groups[j]
                inner = lax.rem(lane, width)
                keep = (inner >= m * each) & (inner < (m + 1) * each) & exists(down, right)
                part = jnp.where(keep, beside[k, j].astype(F32), part)
            parts.append(jnp.where(lane < 4 * width, part, 0.0).astype(BF16))
        around = dot(jnp.concatenate(parts, axis=1), unplace[...])
        for p in range(4):
            side = around[:, p * L : (p + 1) * L] + dot(attacked[k, p], pick[...])
            both = edges(side)
            for t in range(tall):
                spots = slice(t * L, (t + 1) * L)
                block = attacked[k, p, :, spots].astype(F32)
                ends = edge(both, t - RIM)
                attacked_three[p, 0:C, spots] = shifted(block, ends, -1).astype(BF16)
                attacked_three[p, C : 2 * C, spots] = attacked[k, p, :, spots]
                attacked_three[p, 2 * C :, spots] = shifted(block, ends, 1).astype(BF16)
            spots = slice(tall * L, (tall + 1) * L)
            attacked_three[p, 0:C, spots] = pltpu.roll(side, 1, axis=1).astype(BF16)
            attacked_three[p, C : 2 * C, spots] = side.astype(BF16)
            attacked_three[p, 2 * C :, spots] = pltpu.roll(side, L - 1, axis=1).astype(BF16)

    finish(begin)
    attacked_ready(0)
    finish(extra)
    gathered = jnp.zeros((C, L), F32)
    for j, ((down, right), first, pairs) in enumerate(groups):
        keep = (lane >= first) & (lane < first + len(pairs)) & exists(down, right)
        gathered = jnp.where(keep, target_beside[j].astype(F32), gathered)
    target[:, 0 : tall_two * L] = target_main[0, :, 2 * L : (2 + tall_two) * L].astype(F32)
    target[:, tall_two * L :] = dot(gathered.astype(BF16), settle[...]) + dot(
        target_main[0], pick[...]
    )

    def mate_copy(k, g):
        return copy_of(
            grad_sent.at[k, g, 1 - core],
            grad_mate.at[k, g],
            sum_sends.at[k, g, 0],
            sum_recvs.at[k, g, 0],
            mate,
        )

    def peer_copies(ref, index, peers, k, g, at):
        return [
            copy_of(
                ref.at[k, g, index],
                ref.at[k, g, index],
                sum_sends.at[k, g, at + i],
                sum_recvs.at[k, g, at + i],
                device,
            )
            for i, device in enumerate(peers)
        ]

    def plane_copies(k, g):
        return peer_copies(plane, me_plane, plane_peers, k, g, 2)

    def line_copies(k, g):
        return peer_copies(line, far, line_peers, k, g, 2 + len(plane_peers))

    def back_copies(k, g):
        return peer_copies(summed, core, [mate], k, g, 1)

    def begin_sum(k, g, parts):
        for a in range(3):
            grad_wide[g, :, a * C3 : (a + 1) * C3] = parts[a]
        for h in range(2):
            grad[g, h] = grad_wide[g, :, h * H : (h + 1) * H]
            grad_sent[k, g, h] = grad_wide[g, :, h * H : (h + 1) * H].astype(BF16)
        mate_copy(k, g).start()

    def plane_sum(k, g):
        mate_copy(k, g).wait()
        plane[k, g, me_plane] = (grad[g, core] + grad_mate[k, g].astype(F32)).astype(BF16)
        for copy in plane_copies(k, g):
            copy.start()

    def sum_of(ref, k, g, count):
        total = ref[k, g, 0].astype(F32)
        for i in range(1, count):
            total = total + ref[k, g, i].astype(F32)
        return total.astype(BF16)

    def line_sum(k, g):
        for copy in plane_copies(k, g):
            copy.wait()
        line[k, g, far] = sum_of(plane, k, g, 2 * chips)
        for copy in line_copies(k, g):
            copy.start()

    def back_sum(k, g):
        for copy in line_copies(k, g):
            copy.wait()
        summed[k, g, core] = sum_of(line, k, g, lines)
        for copy in back_copies(k, g):
            copy.start()

    def end_sum(k, g):
        for copy in back_copies(k, g):
            copy.wait()
        parts = [summed[k, g, h].astype(F32) for h in range(2)]
        squares = parts[0] * parts[0] + parts[1] * parts[1]
        mean = jnp.sum(jnp.sum(squares, axis=0, keepdims=True), axis=1, keepdims=True) / (K * C)
        scale = jnp.sqrt(mean + mean_epsilon)
        for h in range(2):
            later = momentum_rate * moment[g, :, h * H : (h + 1) * H] + parts[h] / scale
            moment[g, :, h * H : (h + 1) * H] = later
            state[g, :, h * H : (h + 1) * H] -= learn_rate * later

    def replay(k):
        fast_one = [state[0, :, a * C3 : (a + 1) * C3].astype(BF16) for a in range(3)]
        fast_two = [state[1, :, a * C3 : (a + 1) * C3].astype(BF16) for a in range(3)]
        ahead_one = jnp.concatenate(fast_one, axis=0)
        for g in range(2):
            weights[g * C : (g + 1) * C, :] = state[g]
        turned = jnp.transpose(weights[...])
        for i, (a, b) in enumerate(TAPS):
            py, dy = [(1, 1), (0, 0), (1, 0)][a]
            px, dx = [(1, 1), (0, 0), (1, 0)][b]
            block = turned[i * C : (i + 1) * C, :]
            back_wide[a * C : (a + 1) * C, b * C : (b + 1) * C] = block[:, 0:C]
            p, slot = 2 * py + px, 2 * dy + dx
            spread_wide[p * C : (p + 1) * C, slot * C : (slot + 1) * C] = block[:, C : 2 * C]
        spread_weight[...] = spread_wide[:, 0 : 4 * C].astype(BF16)

        for p in (1, 3, 0, 2):
            sums = dot(ahead_one, attacked_three[p])
            main = (
                sums[0:C, 0 : tall_one * L]
                + sums[C : 2 * C, L : (1 + tall_one) * L]
                + sums[2 * C :, 2 * L : (2 + tall_one) * L]
            )
            side = sums[:, tall * L :]
            side = (
                pltpu.roll(side[0:C], PITCH, axis=1)
                + side[C : 2 * C]
                + pltpu.roll(side[2 * C :], L - PITCH, axis=1)
            )
            pre_value = jnp.concatenate([main, side], axis=1)
            sigmoid_value = jax.nn.sigmoid(pre_value)
            value = pre_value * sigmoid_value * inside_one
            slope_value = sigmoid_value * (1.0 + pre_value * (1.0 - sigmoid_value)) * inside_one
            slope[p, :, 0 : tall_three * L] = slope_value[:, L : (1 + tall_three) * L]
            slope[p, :, tall_three * L :] = slope_value[:, tall_one * L :]
            py, px = p // 2, p % 2
            if px == 0:
                hidden_three[py, C : 2 * C, :] = value.astype(BF16)
            else:
                hidden_three[py, 2 * C :, :] = value.astype(BF16)
                side = value[:, tall_one * L :]
                for t in range(tall_one):
                    spots = slice(t * L, (t + 1) * L)
                    moved = shifted(value[:, spots], edge(side, t - 2), -1)
                    hidden_three[py, 0:C, spots] = moved.astype(BF16)
                hidden_three[py, 0:C, tall_one * L :] = pltpu.roll(side, 1, axis=1).astype(BF16)

        outer = dot(jnp.concatenate([fast_two[0], fast_two[2]], axis=0), hidden_three[1])
        middle = dot(fast_two[1], hidden_three[0])
        main = (
            outer[0:C, 0 : tall_two * L]
            + outer[C:, L : (1 + tall_two) * L]
            + middle[:, L : (1 + tall_two) * L]
        )
        side = (
            pltpu.roll(outer[0:C, tall_one * L :], PITCH, axis=1)
            + outer[C:, tall_one * L :]
            + middle[:, tall_one * L :]
        )
        predicted[...] = main[:, L : (1 + rows) * L]
        predict = jnp.concatenate([main, side], axis=1)
        residual = ((predict - target[...]) * inside_two).astype(BF16)
        mine = residual[:, L : (1 + rows) * L]
        begin_sum(
            k,
            1,
            [
                dot_nt(mine, hidden_three[1, :, L : (1 + rows) * L]),
                dot_nt(mine, hidden_three[0, :, 2 * L : (2 + rows) * L]),
                dot_nt(mine, hidden_three[1, :, 2 * L : (2 + rows) * L]),
            ],
        )

        wide = residual.astype(F32)
        side = wide[:, tall_two * L :]
        for t in range(tall_two):
            spot = tiles.side(t - 1, 0)
            first = pltpu.roll(wide[:, t * L : (t + 1) * L], spot, axis=1)
            side = jnp.where(lane == spot, first, side)
        moved = []
        for t in range(tall_two):
            ends = pltpu.roll(side, (L - 1 - tiles.side(t - 1, w)) % L, axis=1)
            moved.append(shifted(wide[:, t * L : (t + 1) * L], ends, 1))
        moved = jnp.concatenate(moved, axis=1)
        moved_side = pltpu.roll(side, L - 1, axis=1)
        for i, (dy, block, beyond) in enumerate(
            ((0, wide, side), (0, moved, moved_side), (1, wide, side), (1, moved, moved_side))
        ):
            part = slice(i * C, (i + 1) * C)
            rest[part, 0 : tall_three * L] = block[:, dy * L : (dy + tall_three) * L].astype(BF16)
            beyond = rolled(beyond, dy * PITCH)
            rest[part, tall_three * L :] = beyond.astype(BF16)
        hidden_grad = dot(spread_weight[...], rest[...])
        plane_sum(k, 1)
        total = jnp.zeros((C3, C3), F32)
        for p in range(4):
            pre_grad = (hidden_grad[p * C : (p + 1) * C, :] * slope[p]).astype(BF16)
            pre[p] = pre_grad
            for a in range(3):
                part = slice(a * C, (a + 1) * C)
                pre_stack[p, part, a * L : (a + rows) * L] = pre_grad[:, L : (1 + rows) * L]
            total = total + dot_nt(pre_stack[p], attacked_three[p, :, 2 * L : (2 + tall_three) * L])
        begin_sum(k, 0, [total[a * C : (a + 1) * C, :] for a in range(3)])

        back_one = back_wide[:, 0:C3].astype(BF16)

        def input_side(p):
            side = pre[p, :, tall_three * L :].astype(F32)
            both = edges(side)
            for t in range(tall_three):
                spots = slice(t * L, (t + 1) * L)
                block = pre[p, :, spots].astype(F32)
                ends = edge(both, t - 1)
                pre_three[0:C, spots] = shifted(block, ends, 1).astype(BF16)
                pre_three[C : 2 * C, spots] = pre[p, :, spots]
                pre_three[2 * C :, spots] = shifted(block, ends, -1).astype(BF16)
            sums = dot(back_one, pre_three[...])
            input_grad = (
                sums[0:C, 2 * L : (2 + rows) * L]
                + sums[C : 2 * C, L : (1 + rows) * L]
                + sums[2 * C :, 0 : rows * L]
            )
            moved = jnp.clip(perturb[p] + step_size * jnp.tanh(input_grad), -clip_bound, clip_bound)
            perturb[p] = moved
            attacked[k + 1, p, :, own] = (image[p].astype(F32) + moved).astype(BF16)

        input_side(0)
        plane_sum(k, 0)
        for p in range(1, 4):
            input_side(p)
        following = rim_of(k + 1)

        @pl.when(k < last)
        def _():
            make_message(k + 1)
            start(following)

        line_sum(k, 1)
        line_sum(k, 0)

        @pl.when(k < last)
        def _():
            finish(following)
            attacked_ready(k + 1)

        @pl.when(k == last)
        def _():
            for r in range(rows):
                spots = slice(r * L, (r + 1) * L)
                rows_short[pl.ds(r, C, stride=rows), :] = predicted[:, spots]
                for py in range(2):
                    for px in range(2):
                        part = perturb[2 * py + px, :, spots]
                        rows_wide[px, pl.ds(2 * r + py, C, stride=high_rows), :] = part
            predict_rows[...] = rows_short[...].astype(BF16)
            back_order = (
                lax.broadcasted_iota(jnp.int32, (2 * w, 2 * w), 1)
                == jnp.where(from_col < w, 2 * from_col, 2 * (from_col - w) + 1)
            ).astype(F32).astype(BF16)
            perturb_rows[...] = dot_exact(rows_wide[0], back_order[:w, :]) + dot_exact(
                rows_wide[1], back_order[w:, :]
            )

        for g in (1, 0):
            back_sum(k, g)
        for g in (1, 0):
            end_sum(k, g)

    @pl.loop(0, REPLAYS)
    def _(k):
        replay(k)


def finish_kernel(channels, *refs):
    perturb_in, predict_in, state, moment = refs[:4]
    outs, held, sems = refs[4:10], refs[10:14], refs[14]
    sources = [perturb_in, predict_in, *held]
    copies = [pltpu.make_async_copy(x, y, sems.at[i]) for i, (x, y) in enumerate(zip(sources, outs))]
    copies[0].start()
    copies[1].start()
    for n, (array, g) in enumerate(((state, 0), (state, 1), (moment, 0), (moment, 1))):
        for i in range(9):
            one, two = i * channels, (i + 1) * channels
            held[n][one:two, :] = array[g, :, one:two]
        copies[2 + n].start()
    for copy in copies:
        copy.wait()


def finished(channels, results):
    perturb, predict = results[:2]
    kernel = (9 * channels, channels)
    shapes = [jax.ShapeDtypeStruct(x.shape, x.dtype) for x in (perturb, predict)]
    shapes += [jax.ShapeDtypeStruct(kernel, F32)] * 4
    return pl.pallas_call(
        functools.partial(finish_kernel, channels),
        out_shape=shapes,
        in_specs=[WHOLE] * 4,
        out_specs=[pl.BlockSpec(memory_space=pl.ANY)] * 6,
        scratch_shapes=[pltpu.VMEM(kernel, F32)] * 4 + [pltpu.SemaphoreType.DMA((6,))],
        compiler_params=pltpu.CompilerParams(vmem_limit_bytes=FINISH_LIMIT),
    )(*results)


def whole(tiles, operands):
    C, H, L = tiles.channels, tiles.half, LANES
    K, C3, rows = 9 * C, 3 * C, tiles.rows
    row_count, col_count = lax.axis_size("rows"), lax.axis_size("cols")
    assert row_count % 2 == 0 and col_count % 2 == 0
    perturb, target = operands[1:3]
    shapes = [
        pltpu.VMEM(perturb.shape, F32),
        pltpu.VMEM(target.shape, BF16),
    ] + [pltpu.VMEM((2, C, 2 * H), F32)] * 2
    sums = 2 + (row_count - 1) + (col_count // 2 - 1)
    scratch = [pltpu.VMEM(x.shape, x.dtype) for x in operands] + [
        pltpu.VMEM((REPLAYS + 1, 4, C, tiles.tall * L), BF16),
        pltpu.VMEM((4, C3, tiles.total), BF16),
        pltpu.VMEM((4, C, (rows + 3) * L), F32),
        pltpu.VMEM((2, C3, (rows + 5) * L), BF16),
        pltpu.VMEM((4 * C, (rows + 3) * L), BF16),
        pltpu.VMEM((4, C, (rows + 3) * L), BF16),
        pltpu.VMEM((4, C3, (rows + 2) * L), BF16),
        pltpu.VMEM((C3, (rows + 2) * L), BF16),
        pltpu.VMEM((4, C, rows * L), BF16),
        pltpu.VMEM((4, C, rows * L), F32),
        pltpu.VMEM((1, C, tiles.tall * L), BF16),
        pltpu.VMEM((C, (rows + 4) * L), F32),
        pltpu.VMEM((C, rows * L), F32),
        pltpu.VMEM((REPLAYS, 4, C, L), BF16),
        pltpu.VMEM((C, L), BF16),
        pltpu.VMEM((REPLAYS, len(SIDES), C, L), BF16),
        pltpu.VMEM((len(SIDES), C, L), BF16),
        pltpu.VMEM((L, 2 * H), F32),
        pltpu.VMEM((C3, 2 * L), F32),
        pltpu.VMEM((4 * C, 2 * L), F32),
        pltpu.VMEM((4 * C, 4 * C), BF16),
        pltpu.VMEM((2, C, 2 * H), F32),
        pltpu.VMEM((2, 2, C, H), F32),
        pltpu.VMEM((REPLAYS, 2, 2, C, H), BF16),
        pltpu.VMEM((REPLAYS, 2, C, H), BF16),
        pltpu.VMEM((REPLAYS, 2, row_count, C, H), BF16),
        pltpu.VMEM((REPLAYS, 2, col_count // 2, C, H), BF16),
        pltpu.VMEM((REPLAYS, 2, 2, C, H), BF16),
        pltpu.SemaphoreType.DMA((len(operands),)),
        pltpu.SemaphoreType.DMA((REPLAYS + 1, 8)),
        pltpu.SemaphoreType.DMA((REPLAYS + 1, 8)),
        pltpu.SemaphoreType.DMA((REPLAYS, 2, sums)),
        pltpu.SemaphoreType.DMA((REPLAYS, 2, sums)),
        pltpu.VMEM((2, perturb.shape[0], L), F32),
        pltpu.VMEM(target.shape, F32),
    ]
    return pl.pallas_call(
        functools.partial(whole_kernel, tiles, row_count, col_count),
        out_shape=shapes,
        in_specs=[pl.BlockSpec(memory_space=pltpu.HBM)] * len(operands),
        out_specs=[WHOLE] * len(shapes),
        scratch_shapes=scratch,
        compiler_params=pltpu.CompilerParams(
            collective_id=0, has_side_effects=True, vmem_limit_bytes=VMEM_LIMIT
        ),
    )(*operands)


def body(image, perturb, target, *kernels):
    C = image.shape[0]
    tiles = Tiles(C, target.shape[1], target.shape[2])
    tables = [jnp.asarray(t) for t in tiles.tables()]
    merged = [x.reshape(-1, x.shape[2]) for x in (image, perturb, target)]
    kernels = [x.transpose(2, 3, 0, 1).reshape(9 * C, C) for x in kernels]
    results = whole(tiles, merged + tables + kernels)
    new_perturb, prediction, *kernels = finished(C, results)
    kernels = [x.reshape(3, 3, C, C).transpose(2, 3, 0, 1) for x in kernels]
    return (new_perturb.reshape(perturb.shape), prediction.reshape(target.shape), *kernels)


def solution(mesh):
    block = P(None, "rows", "cols")
    in_specs = (block, block, block, P(), P(), P(), P())
    out_specs = (block, block, P(), P(), P(), P())
    return jax.shard_map(body, mesh=mesh, in_specs=in_specs, out_specs=out_specs, check_vma=False)
```

```python
import functools

import jax
import jax.numpy as jnp
import ml_dtypes
import numpy as np
from jax import lax
from jax.experimental import pallas as pl
from jax.experimental.pallas import tpu as pltpu
from jax.sharding import PartitionSpec as P

REPLAYS = 3

step_size = 0.5
clip_bound = 0.5
momentum_rate = 0.9
learn_rate = 0.005
mean_epsilon = 1e-06

MESH = pl.DeviceIdType.MESH
BF16 = jnp.bfloat16
F32 = jnp.float32
RIM = 3
LANES = 128
VMEM_LIMIT = 56 * 1024 * 1024
FINISH_LIMIT = 16 * 1024 * 1024
WHOLE = pl.BlockSpec(memory_space=pltpu.VMEM)

SIDES = ((0, -1), (0, 1), (-1, -1), (-1, 1), (1, -1), (1, 1))
TAPS = [(a, b) for a in range(3) for b in range(3)]


SIDE_COLS = (-3, -2, -1, 0)
PITCH = 9


class Tiles:
    def __init__(self, channels, rows, cols):
        self.channels, self.rows, self.cols = channels, rows, cols
        self.tall = rows + 2 * RIM
        self.total = (self.tall + 1) * LANES
        self.half = -(-9 * channels // (2 * LANES)) * LANES
        assert cols == LANES and self.tall * PITCH <= LANES
        groups = self.places()
        self.families = []
        for members in ((0,), (1,), (2, 3), (4, 5)):
            low = groups[members[0]][1]
            width = sum(len(groups[j][2]) for j in members)
            assert 4 * width <= LANES
            self.families.append((members, low, width))

    def side(self, row, col):
        return (row + RIM) * PITCH + (col + RIM if col <= 0 else col - self.cols + 6)

    def places(self):
        groups = []
        lane = 0
        for down, right in SIDES:
            rows = {0: range(self.rows), -1: range(self.rows - RIM, self.rows), 1: range(RIM)}[down]
            cols = {-1: range(self.cols - RIM, self.cols), 1: range(RIM)}[right]
            pairs = [(r, c) for r in rows for c in cols]
            groups.append(((down, right), lane, pairs))
            lane += len(pairs)
        assert lane <= LANES
        return groups

    def tables(self):
        kind = ml_dtypes.bfloat16
        pack = np.zeros((self.rows * LANES, LANES), kind)
        settle = np.zeros((LANES, LANES), kind)
        for (down, right), lane, pairs in self.places():
            for k, (r, c) in enumerate(pairs):
                pack[r * LANES + c, lane + k] = 1
                settle[lane + k, self.side(r + down * self.rows, c + right * self.cols)] = 1
        place = np.zeros((4, LANES, 4 * LANES), kind)
        unplace = np.zeros((4 * LANES, 4 * LANES), kind)
        for f, (_, low, width) in enumerate(self.families):
            for p in range(4):
                for i in range(width):
                    spot = f * LANES + p * width + i
                    place[p, low + i, spot] = 1
                    unplace[spot, p * LANES : (p + 1) * LANES] = settle[low + i]
        pick = np.zeros((self.tall * LANES, LANES), kind)
        where = np.zeros((8, self.total), np.int32)
        where[0, :] = -(10**6)
        for t in range(self.tall):
            where[0, t * LANES : (t + 1) * LANES] = t - RIM
            where[1, t * LANES : (t + 1) * LANES] = np.arange(LANES)
            for col in (0, self.cols - 2, self.cols - 1):
                pick[t * LANES + col, self.side(t - RIM, col)] = 1
            for col in SIDE_COLS + tuple(range(self.cols - 2, self.cols + RIM)):
                spot = self.tall * LANES + self.side(t - RIM, col)
                where[0, spot], where[1, spot] = t - RIM, col
        return pack, place, unplace, settle, pick, where


def dot(a, b):
    return jnp.dot(a, b, preferred_element_type=F32)


def dot_nt(a, b):
    return lax.dot_general(a, b, (((1,), (1,)), ((), ())), preferred_element_type=F32)


def dot_exact(values, table):
    high = values.astype(BF16)
    rest = values - high.astype(F32)
    middle = rest.astype(BF16)
    low = (rest - middle.astype(F32)).astype(BF16)
    return dot(high, table) + (dot(middle, table) + dot(low, table))


def rolled(values, shift):
    if shift % values.shape[1] == 0:
        return values
    return pltpu.roll(values, (-shift) % values.shape[1], axis=1)


def whole_kernel(tiles, row_count, col_count, *refs):
    sources = refs[:13]
    (perturb_rows, predict_rows, state, moment) = refs[13:17]
    held = refs[17:30]
    (image_in, perturb_in, target_in, pack, place, unplace, settle, pick, where) = held[:9]
    (k1_in, k2_in, m1_in, m2_in) = held[9:]
    (
        attacked, attacked_three, slope, hidden_three, rest, pre, pre_stack, pre_three,
        image, perturb, target_main, target, predicted,
        message, target_message, beside, target_beside,
        weights, back_wide, spread_wide, spread_weight,
        grad_wide, grad, grad_sent, grad_mate, plane, line, summed,
        load_sems, rim_sends, rim_recvs, sum_sends, sum_recvs, rows_wide, rows_short,
    ) = refs[30:]
    C, H, L, tall = tiles.channels, tiles.half, LANES, tiles.tall
    K, C3 = 9 * C, 3 * C
    rows, w = tiles.rows, tiles.cols
    own = slice(RIM * L, (RIM + rows) * L)
    me_row, me_col = lax.axis_index("rows"), lax.axis_index("cols")
    core, chip = lax.rem(me_row, 2), me_row // 2
    near, far = lax.rem(me_col, 2), me_col // 2
    chips, lines = row_count // 2, col_count // 2
    me_plane = chip * 2 + near
    last = REPLAYS - 1

    def exists(down, right):
        return (
            (me_row + down >= 0)
            & (me_row + down < row_count)
            & (me_col + right >= 0)
            & (me_col + right < col_count)
        )

    mate = {"rows": me_row + 1 - 2 * core, "cols": me_col}
    plane_peers = []
    for dx in range(chips):
        for dy in range(2):
            if dx or dy:
                there = lax.rem(chip + dx, chips) * 2 + core
                plane_peers.append({"rows": there, "cols": far * 2 + lax.rem(near + dy, 2)})
    line_peers = [
        {"rows": me_row, "cols": lax.rem(far + d, lines) * 2 + near} for d in range(1, lines)
    ]

    barrier = pltpu.get_barrier_semaphore()

    def signal(device):
        pl.semaphore_signal(barrier, inc=1, device_id=device, device_id_type=MESH)

    greeted = 1 + len(plane_peers) + len(line_peers)
    for device in line_peers + plane_peers + [mate]:
        signal(device)
    for down, right in SIDES + ((1, 0), (-1, 0)):
        there = exists(down, right)
        pl.when(there)(
            functools.partial(signal, {"rows": me_row + down, "cols": me_col + right})
        )
        greeted = greeted + there.astype(jnp.int32)

    loads = [
        pltpu.make_async_copy(source, target, load_sems.at[i])
        for i, (source, target) in enumerate(zip(sources, held))
    ]
    for load in loads:
        load.start()

    lane = lax.broadcasted_iota(jnp.int32, (1, L), 1)

    @pl.when(me_row == 0)
    def _():
        for k in range(REPLAYS):
            attacked[k, :, :, 0 : RIM * L] = jnp.zeros((4, C, RIM * L), BF16)
        target_main[0, :, 0 : RIM * L] = jnp.zeros((C, RIM * L), BF16)

    @pl.when(me_row == row_count - 1)
    def _():
        for k in range(REPLAYS):
            attacked[k, :, :, (RIM + rows) * L :] = jnp.zeros((4, C, RIM * L), BF16)
        target_main[0, :, (RIM + rows) * L :] = jnp.zeros((C, RIM * L), BF16)

    from_col = lax.broadcasted_iota(jnp.int32, (2 * w, 2 * w), 0)
    to_col = lax.broadcasted_iota(jnp.int32, (2 * w, 2 * w), 1)
    sorted_from = jnp.where(to_col < w, 2 * to_col, 2 * (to_col - w) + 1)
    order = (from_col == sorted_from).astype(F32).astype(BF16)
    high_rows = 2 * rows

    def spread_rows(parts, put):
        rows_wide[0] = parts[:, :w]
        rows_wide[1] = parts[:, w:]
        for r in range(rows):
            for py in range(2):
                for px in range(2):
                    part = rows_wide[px, pl.ds(2 * r + py, C, stride=high_rows), :]
                    put(2 * py + px, slice(r * L, (r + 1) * L), part)

    def put_image(p, spots, part):
        image[p, :, spots] = part.astype(BF16)

    def put_perturb(p, spots, part):
        perturb[p, :, spots] = part

    loads[0].wait()
    spread_rows(dot(image_in[...], order), put_image)
    loads[1].wait()
    spread_rows(dot_exact(perturb_in[...], order), put_perturb)
    for p in range(4):
        attacked[0, p, :, own] = (image[p].astype(F32) + perturb[p]).astype(BF16)
    loads[2].wait()
    rows_short[...] = target_in[...].astype(F32)
    for r in range(rows):
        spot = (RIM + r) * L
        target_main[0, :, spot : spot + L] = rows_short[pl.ds(r, C, stride=rows), :].astype(BF16)

    def make_message(k):
        phases = [dot(attacked[k, p, :, own], pack[...]).astype(BF16) for p in range(4)]
        total = dot(phases[0], place[0])
        for p in range(1, 4):
            total = total + dot(phases[p], place[p])
        for f in range(4):
            message[k, f] = total[:, f * L : (f + 1) * L].astype(BF16)

    loads[3].wait()
    loads[4].wait()
    make_message(0)
    target_message[...] = dot(target_main[0, :, own], pack[...]).astype(BF16)
    pl.semaphore_wait(barrier, greeted)

    def copy_of(source, target, sends, recvs, device):
        return pltpu.make_async_remote_copy(
            src_ref=source,
            dst_ref=target,
            send_sem=sends,
            recv_sem=recvs,
            device_id=device,
            device_id_type=MESH,
        )

    family_of = {j: f for f, (members, _, _) in enumerate(tiles.families) for j in members}

    def rim_copies(block, sides, to_beside, k):
        copies = []

        def add(source, target, down, right):
            i = len(copies)
            device = {"rows": me_row + down, "cols": me_col + right}
            copy = copy_of(source, target, rim_sends.at[k, i], rim_recvs.at[k, i], device)
            copies.append((copy, exists(down, right), exists(-down, -right)))

        for j, (down, right) in enumerate(SIDES):
            add(sides(j), to_beside.at[j], -down, -right)
        deep = RIM * L
        add(block.at[:, :, pl.ds(rows * L, deep)], block.at[:, :, pl.ds(0, deep)], 1, 0)
        add(block.at[:, :, pl.ds(deep, deep)], block.at[:, :, pl.ds(deep + rows * L, deep)], -1, 0)
        return copies

    def start(copies):
        for copy, there, _ in copies:
            pl.when(there)(copy.start)

    def finish(copies):
        for copy, there, here in copies:
            pl.when(there)(copy.wait_send)
            pl.when(here)(copy.wait_recv)

    def rim_of(k):
        return rim_copies(attacked.at[k], lambda j: message.at[k, family_of[j]], beside.at[k], k)

    begin = rim_of(0)
    start(begin)
    extra = rim_copies(target_main, lambda j: target_message, target_beside, REPLAYS)
    start(extra)

    for load in loads[5:]:
        load.wait()
    far_row, far_col = where[0:1, :] + me_row * rows, where[1:2, :] + me_col * w
    inside = (
        (far_row >= 0)
        & (far_row < rows * row_count)
        & (far_col >= 0)
        & (far_col < w * col_count)
    ).astype(F32)
    inside_side = inside[:, tall * L :]
    tall_one, tall_two, tall_three = rows + 4, rows + 3, rows + 2
    inside_one = jnp.concatenate([inside[:, L : (1 + tall_one) * L], inside_side], axis=1)
    inside_two = jnp.concatenate([inside[:, 2 * L : (2 + tall_two) * L], inside_side], axis=1)

    state[...] = jnp.zeros(state.shape, F32)
    moment[...] = jnp.zeros(moment.shape, F32)
    grad_wide[...] = jnp.zeros(grad_wide.shape, F32)
    weights[...] = jnp.zeros(weights.shape, F32)
    spread_wide[...] = jnp.zeros(spread_wide.shape, F32)
    pre_stack[...] = jnp.zeros(pre_stack.shape, BF16)
    for i in range(9):
        one, two = i * C, (i + 1) * C
        state[0, :, one:two] = k1_in[one:two, :]
        state[1, :, one:two] = k2_in[one:two, :]
        moment[0, :, one:two] = m1_in[one:two, :]
        moment[1, :, one:two] = m2_in[one:two, :]

    groups = tiles.places()
    slot_of = lax.rem(lane, PITCH)

    def shifted(block, edge, by):
        end = 0 if by < 0 else L - 1
        return jnp.where(lane == end, edge, pltpu.roll(block, (-by) % L, axis=1))

    def edges(side):
        return jnp.where(slot_of == 2, side, pltpu.roll(side, L - 5, axis=1))

    def edge(both, row):
        return pltpu.roll(both, (-tiles.side(row, -1)) % L, axis=1)

    def attacked_ready(k):
        parts = []
        for members, _, width in tiles.families:
            part = jnp.zeros((C, L), F32)
            each = width // len(members)
            for m, j in enumerate(members):
                (down, right), _, _ = groups[j]
                inner = lax.rem(lane, width)
                keep = (inner >= m * each) & (inner < (m + 1) * each) & exists(down, right)
                part = jnp.where(keep, beside[k, j].astype(F32), part)
            parts.append(jnp.where(lane < 4 * width, part, 0.0).astype(BF16))
        around = dot(jnp.concatenate(parts, axis=1), unplace[...])
        for p in range(4):
            side = around[:, p * L : (p + 1) * L] + dot(attacked[k, p], pick[...])
            both = edges(side)
            for t in range(tall):
                spots = slice(t * L, (t + 1) * L)
                block = attacked[k, p, :, spots].astype(F32)
                ends = edge(both, t - RIM)
                attacked_three[p, 0:C, spots] = shifted(block, ends, -1).astype(BF16)
                attacked_three[p, C : 2 * C, spots] = attacked[k, p, :, spots]
                attacked_three[p, 2 * C :, spots] = shifted(block, ends, 1).astype(BF16)
            spots = slice(tall * L, (tall + 1) * L)
            attacked_three[p, 0:C, spots] = pltpu.roll(side, 1, axis=1).astype(BF16)
            attacked_three[p, C : 2 * C, spots] = side.astype(BF16)
            attacked_three[p, 2 * C :, spots] = pltpu.roll(side, L - 1, axis=1).astype(BF16)

    finish(begin)
    attacked_ready(0)
    finish(extra)
    gathered = jnp.zeros((C, L), F32)
    for j, ((down, right), first, pairs) in enumerate(groups):
        keep = (lane >= first) & (lane < first + len(pairs)) & exists(down, right)
        gathered = jnp.where(keep, target_beside[j].astype(F32), gathered)
    target[:, 0 : tall_two * L] = target_main[0, :, 2 * L : (2 + tall_two) * L].astype(F32)
    target[:, tall_two * L :] = dot(gathered.astype(BF16), settle[...]) + dot(
        target_main[0], pick[...]
    )

    def mate_copy(k, g):
        return copy_of(
            grad_sent.at[k, g, 1 - core],
            grad_mate.at[k, g],
            sum_sends.at[k, g, 0],
            sum_recvs.at[k, g, 0],
            mate,
        )

    def peer_copies(ref, index, peers, k, g, at):
        return [
            copy_of(
                ref.at[k, g, index],
                ref.at[k, g, index],
                sum_sends.at[k, g, at + i],
                sum_recvs.at[k, g, at + i],
                device,
            )
            for i, device in enumerate(peers)
        ]

    def plane_copies(k, g):
        return peer_copies(plane, me_plane, plane_peers, k, g, 2)

    def line_copies(k, g):
        return peer_copies(line, far, line_peers, k, g, 2 + len(plane_peers))

    def back_copies(k, g):
        return peer_copies(summed, core, [mate], k, g, 1)

    def begin_sum(k, g, parts):
        for a in range(3):
            grad_wide[g, :, a * C3 : (a + 1) * C3] = parts[a]
        for h in range(2):
            grad[g, h] = grad_wide[g, :, h * H : (h + 1) * H]
            grad_sent[k, g, h] = grad_wide[g, :, h * H : (h + 1) * H].astype(BF16)
        mate_copy(k, g).start()

    def plane_sum(k, g):
        mate_copy(k, g).wait()
        plane[k, g, me_plane] = (grad[g, core] + grad_mate[k, g].astype(F32)).astype(BF16)
        for copy in plane_copies(k, g):
            copy.start()

    def sum_of(ref, k, g, count):
        total = ref[k, g, 0].astype(F32)
        for i in range(1, count):
            total = total + ref[k, g, i].astype(F32)
        return total.astype(BF16)

    def line_sum(k, g):
        for copy in plane_copies(k, g):
            copy.wait()
        line[k, g, far] = sum_of(plane, k, g, 2 * chips)
        for copy in line_copies(k, g):
            copy.start()

    def back_sum(k, g):
        for copy in line_copies(k, g):
            copy.wait()
        summed[k, g, core] = sum_of(line, k, g, lines)
        for copy in back_copies(k, g):
            copy.start()

    def end_sum(k, g):
        for copy in back_copies(k, g):
            copy.wait()
        parts = [summed[k, g, h].astype(F32) for h in range(2)]
        squares = parts[0] * parts[0] + parts[1] * parts[1]
        mean = jnp.sum(jnp.sum(squares, axis=0, keepdims=True), axis=1, keepdims=True) / (K * C)
        unit = 1.0 / jnp.sqrt(mean + mean_epsilon)
        for h in range(2):
            later = momentum_rate * moment[g, :, h * H : (h + 1) * H] + parts[h] * unit
            moment[g, :, h * H : (h + 1) * H] = later
            state[g, :, h * H : (h + 1) * H] -= learn_rate * later

    def turned(g):
        weights[0:C, :] = state[g]
        return jnp.transpose(weights[...])

    def spread_ready():
        wide = turned(1)
        for i, (a, b) in enumerate(TAPS):
            py, dy = [(1, 1), (0, 0), (1, 0)][a]
            px, dx = [(1, 1), (0, 0), (1, 0)][b]
            p, slot = 2 * py + px, 2 * dy + dx
            block = wide[i * C : (i + 1) * C, 0:C]
            spread_wide[p * C : (p + 1) * C, slot * C : (slot + 1) * C] = block
        spread_weight[...] = spread_wide[:, 0 : 4 * C].astype(BF16)

    def back_ready():
        wide = turned(0)
        for i, (a, b) in enumerate(TAPS):
            block = wide[i * C : (i + 1) * C, 0:C]
            back_wide[a * C : (a + 1) * C, b * C : (b + 1) * C] = block
        return back_wide[:, 0:C3].astype(BF16)

    spread_ready()

    def replay(k):
        fast_one = [state[0, :, a * C3 : (a + 1) * C3].astype(BF16) for a in range(3)]
        fast_two = [state[1, :, a * C3 : (a + 1) * C3].astype(BF16) for a in range(3)]
        ahead_one = jnp.concatenate(fast_one, axis=0)
        for p in (1, 3, 0, 2):
            sums = dot(ahead_one, attacked_three[p])
            main = (
                sums[0:C, 0 : tall_one * L]
                + sums[C : 2 * C, L : (1 + tall_one) * L]
                + sums[2 * C :, 2 * L : (2 + tall_one) * L]
            )
            side = sums[:, tall * L :]
            side = (
                pltpu.roll(side[0:C], PITCH, axis=1)
                + side[C : 2 * C]
                + pltpu.roll(side[2 * C :], L - PITCH, axis=1)
            )
            pre_value = jnp.concatenate([main, side], axis=1)
            sigmoid_value = jax.nn.sigmoid(pre_value)
            value = pre_value * sigmoid_value * inside_one
            slope_value = sigmoid_value * (1.0 + pre_value * (1.0 - sigmoid_value)) * inside_one
            slope[p, :, 0 : tall_three * L] = slope_value[:, L : (1 + tall_three) * L]
            slope[p, :, tall_three * L :] = slope_value[:, tall_one * L :]
            py, px = p // 2, p % 2
            if px == 0:
                hidden_three[py, C : 2 * C, :] = value.astype(BF16)
            else:
                hidden_three[py, 2 * C :, :] = value.astype(BF16)
                side = value[:, tall_one * L :]
                for t in range(tall_one):
                    spots = slice(t * L, (t + 1) * L)
                    moved = shifted(value[:, spots], edge(side, t - 2), -1)
                    hidden_three[py, 0:C, spots] = moved.astype(BF16)
                hidden_three[py, 0:C, tall_one * L :] = pltpu.roll(side, 1, axis=1).astype(BF16)

        outer = dot(jnp.concatenate([fast_two[0], fast_two[2]], axis=0), hidden_three[1])
        middle = dot(fast_two[1], hidden_three[0])
        main = (
            outer[0:C, 0 : tall_two * L]
            + outer[C:, L : (1 + tall_two) * L]
            + middle[:, L : (1 + tall_two) * L]
        )
        side = (
            pltpu.roll(outer[0:C, tall_one * L :], PITCH, axis=1)
            + outer[C:, tall_one * L :]
            + middle[:, tall_one * L :]
        )
        predicted[...] = main[:, L : (1 + rows) * L]
        predict = jnp.concatenate([main, side], axis=1)
        residual = ((predict - target[...]) * inside_two).astype(BF16)
        mine = residual[:, L : (1 + rows) * L]
        begin_sum(
            k,
            1,
            [
                dot_nt(mine, hidden_three[1, :, L : (1 + rows) * L]),
                dot_nt(mine, hidden_three[0, :, 2 * L : (2 + rows) * L]),
                dot_nt(mine, hidden_three[1, :, 2 * L : (2 + rows) * L]),
            ],
        )

        wide = residual.astype(F32)
        side = wide[:, tall_two * L :]
        for t in range(tall_two):
            spot = tiles.side(t - 1, 0)
            first = pltpu.roll(wide[:, t * L : (t + 1) * L], spot, axis=1)
            side = jnp.where(lane == spot, first, side)
        moved = []
        for t in range(tall_two):
            ends = pltpu.roll(side, (L - 1 - tiles.side(t - 1, w)) % L, axis=1)
            moved.append(shifted(wide[:, t * L : (t + 1) * L], ends, 1))
        moved = jnp.concatenate(moved, axis=1)
        moved_side = pltpu.roll(side, L - 1, axis=1)
        for i, (dy, block, beyond) in enumerate(
            ((0, wide, side), (0, moved, moved_side), (1, wide, side), (1, moved, moved_side))
        ):
            part = slice(i * C, (i + 1) * C)
            rest[part, 0 : tall_three * L] = block[:, dy * L : (dy + tall_three) * L].astype(BF16)
            beyond = rolled(beyond, dy * PITCH)
            rest[part, tall_three * L :] = beyond.astype(BF16)
        hidden_grad = dot(spread_weight[...], rest[...])
        total = jnp.zeros((C3, C3), F32)
        for p in range(4):
            if p == 2:
                plane_sum(k, 1)
            pre_grad = (hidden_grad[p * C : (p + 1) * C, :] * slope[p]).astype(BF16)
            pre[p] = pre_grad
            for a in range(3):
                part = slice(a * C, (a + 1) * C)
                pre_stack[p, part, a * L : (a + rows) * L] = pre_grad[:, L : (1 + rows) * L]
            total = total + dot_nt(pre_stack[p], attacked_three[p, :, 2 * L : (2 + tall_three) * L])
        begin_sum(k, 0, [total[a * C : (a + 1) * C, :] for a in range(3)])

        back_one = back_ready()

        def input_side(p):
            side = pre[p, :, tall_three * L :].astype(F32)
            both = edges(side)
            for t in range(tall_three):
                spots = slice(t * L, (t + 1) * L)
                block = pre[p, :, spots].astype(F32)
                ends = edge(both, t - 1)
                pre_three[0:C, spots] = shifted(block, ends, 1).astype(BF16)
                pre_three[C : 2 * C, spots] = pre[p, :, spots]
                pre_three[2 * C :, spots] = shifted(block, ends, -1).astype(BF16)
            sums = dot(back_one, pre_three[...])
            input_grad = (
                sums[0:C, 2 * L : (2 + rows) * L]
                + sums[C : 2 * C, L : (1 + rows) * L]
                + sums[2 * C :, 0 : rows * L]
            )
            moved = jnp.clip(perturb[p] + step_size * jnp.tanh(input_grad), -clip_bound, clip_bound)
            perturb[p] = moved
            attacked[k + 1, p, :, own] = (image[p].astype(F32) + moved).astype(BF16)

        input_side(0)
        plane_sum(k, 0)
        for p in range(1, 4):
            input_side(p)
        following = rim_of(k + 1)

        @pl.when(k < last)
        def _():
            make_message(k + 1)
            start(following)

        line_sum(k, 1)
        line_sum(k, 0)

        @pl.when(k < last)
        def _():
            finish(following)
            attacked_ready(k + 1)

        @pl.when(k == last)
        def _():
            for r in range(rows):
                spots = slice(r * L, (r + 1) * L)
                rows_short[pl.ds(r, C, stride=rows), :] = predicted[:, spots]
                for py in range(2):
                    for px in range(2):
                        part = perturb[2 * py + px, :, spots]
                        rows_wide[px, pl.ds(2 * r + py, C, stride=high_rows), :] = part
            predict_rows[...] = rows_short[...].astype(BF16)
            back_order = (
                lax.broadcasted_iota(jnp.int32, (2 * w, 2 * w), 1)
                == jnp.where(from_col < w, 2 * from_col, 2 * (from_col - w) + 1)
            ).astype(F32).astype(BF16)
            perturb_rows[...] = dot_exact(rows_wide[0], back_order[:w, :]) + dot_exact(
                rows_wide[1], back_order[w:, :]
            )

        for g in (1, 0):
            back_sum(k, g)
        end_sum(k, 1)
        spread_ready()
        end_sum(k, 0)

    @pl.loop(0, REPLAYS)
    def _(k):
        replay(k)


def finish_kernel(channels, *refs):
    perturb_in, predict_in, state, moment = refs[:4]
    outs, held, sems = refs[4:10], refs[10:14], refs[14]
    sources = [perturb_in, predict_in, *held]
    copies = [pltpu.make_async_copy(x, y, sems.at[i]) for i, (x, y) in enumerate(zip(sources, outs))]
    copies[0].start()
    copies[1].start()
    for n, (array, g) in enumerate(((state, 0), (state, 1), (moment, 0), (moment, 1))):
        for i in range(9):
            one, two = i * channels, (i + 1) * channels
            held[n][one:two, :] = array[g, :, one:two]
        copies[2 + n].start()
    for copy in copies:
        copy.wait()


def finished(channels, results):
    perturb, predict = results[:2]
    kernel = (9 * channels, channels)
    shapes = [jax.ShapeDtypeStruct(x.shape, x.dtype) for x in (perturb, predict)]
    shapes += [jax.ShapeDtypeStruct(kernel, F32)] * 4
    return pl.pallas_call(
        functools.partial(finish_kernel, channels),
        out_shape=shapes,
        in_specs=[WHOLE] * 4,
        out_specs=[pl.BlockSpec(memory_space=pl.ANY)] * 6,
        scratch_shapes=[pltpu.VMEM(kernel, F32)] * 4 + [pltpu.SemaphoreType.DMA((6,))],
        compiler_params=pltpu.CompilerParams(vmem_limit_bytes=FINISH_LIMIT),
    )(*results)


def whole(tiles, operands):
    C, H, L = tiles.channels, tiles.half, LANES
    K, C3, rows = 9 * C, 3 * C, tiles.rows
    row_count, col_count = lax.axis_size("rows"), lax.axis_size("cols")
    assert row_count % 2 == 0 and col_count % 2 == 0
    perturb, target = operands[1:3]
    shapes = [
        pltpu.VMEM(perturb.shape, F32),
        pltpu.VMEM(target.shape, BF16),
    ] + [pltpu.VMEM((2, C, 2 * H), F32)] * 2
    sums = 2 + (row_count - 1) + (col_count // 2 - 1)
    scratch = [pltpu.VMEM(x.shape, x.dtype) for x in operands] + [
        pltpu.VMEM((REPLAYS + 1, 4, C, tiles.tall * L), BF16),
        pltpu.VMEM((4, C3, tiles.total), BF16),
        pltpu.VMEM((4, C, (rows + 3) * L), F32),
        pltpu.VMEM((2, C3, (rows + 5) * L), BF16),
        pltpu.VMEM((4 * C, (rows + 3) * L), BF16),
        pltpu.VMEM((4, C, (rows + 3) * L), BF16),
        pltpu.VMEM((4, C3, (rows + 2) * L), BF16),
        pltpu.VMEM((C3, (rows + 2) * L), BF16),
        pltpu.VMEM((4, C, rows * L), BF16),
        pltpu.VMEM((4, C, rows * L), F32),
        pltpu.VMEM((1, C, tiles.tall * L), BF16),
        pltpu.VMEM((C, (rows + 4) * L), F32),
        pltpu.VMEM((C, rows * L), F32),
        pltpu.VMEM((REPLAYS, 4, C, L), BF16),
        pltpu.VMEM((C, L), BF16),
        pltpu.VMEM((REPLAYS, len(SIDES), C, L), BF16),
        pltpu.VMEM((len(SIDES), C, L), BF16),
        pltpu.VMEM((L, 2 * H), F32),
        pltpu.VMEM((C3, 2 * L), F32),
        pltpu.VMEM((4 * C, 2 * L), F32),
        pltpu.VMEM((4 * C, 4 * C), BF16),
        pltpu.VMEM((2, C, 2 * H), F32),
        pltpu.VMEM((2, 2, C, H), F32),
        pltpu.VMEM((REPLAYS, 2, 2, C, H), BF16),
        pltpu.VMEM((REPLAYS, 2, C, H), BF16),
        pltpu.VMEM((REPLAYS, 2, row_count, C, H), BF16),
        pltpu.VMEM((REPLAYS, 2, col_count // 2, C, H), BF16),
        pltpu.VMEM((REPLAYS, 2, 2, C, H), BF16),
        pltpu.SemaphoreType.DMA((len(operands),)),
        pltpu.SemaphoreType.DMA((REPLAYS + 1, 8)),
        pltpu.SemaphoreType.DMA((REPLAYS + 1, 8)),
        pltpu.SemaphoreType.DMA((REPLAYS, 2, sums)),
        pltpu.SemaphoreType.DMA((REPLAYS, 2, sums)),
        pltpu.VMEM((2, perturb.shape[0], L), F32),
        pltpu.VMEM(target.shape, F32),
    ]
    return pl.pallas_call(
        functools.partial(whole_kernel, tiles, row_count, col_count),
        out_shape=shapes,
        in_specs=[pl.BlockSpec(memory_space=pltpu.HBM)] * len(operands),
        out_specs=[WHOLE] * len(shapes),
        scratch_shapes=scratch,
        compiler_params=pltpu.CompilerParams(
            collective_id=0, has_side_effects=True, vmem_limit_bytes=VMEM_LIMIT
        ),
    )(*operands)


def body(image, perturb, target, *kernels):
    C = image.shape[0]
    tiles = Tiles(C, target.shape[1], target.shape[2])
    tables = [jnp.asarray(t) for t in tiles.tables()]
    merged = [x.reshape(-1, x.shape[2]) for x in (image, perturb, target)]
    kernels = [x.transpose(2, 3, 0, 1).reshape(9 * C, C) for x in kernels]
    results = whole(tiles, merged + tables + kernels)
    new_perturb, prediction, *kernels = finished(C, results)
    kernels = [x.reshape(3, 3, C, C).transpose(2, 3, 0, 1) for x in kernels]
    return (new_perturb.reshape(perturb.shape), prediction.reshape(target.shape), *kernels)


def solution(mesh):
    block = P(None, "rows", "cols")
    in_specs = (block, block, block, P(), P(), P(), P())
    out_specs = (block, block, P(), P(), P(), P())
    return jax.shard_map(body, mesh=mesh, in_specs=in_specs, out_specs=out_specs, check_vma=False)
```

```python
import functools

import jax
import jax.numpy as jnp
import ml_dtypes
import numpy as np
from jax import lax
from jax.experimental import pallas as pl
from jax.experimental.pallas import tpu as pltpu
from jax.sharding import PartitionSpec as P

REPLAYS = 3

step_size = 0.5
clip_bound = 0.5
momentum_rate = 0.9
learn_rate = 0.005
mean_epsilon = 1e-06

MESH = pl.DeviceIdType.MESH
BF16 = jnp.bfloat16
F32 = jnp.float32
RIM = 3
LANES = 128
VMEM_LIMIT = 56 * 1024 * 1024
FINISH_LIMIT = 16 * 1024 * 1024
WHOLE = pl.BlockSpec(memory_space=pltpu.VMEM)

SIDES = ((0, -1), (0, 1), (-1, -1), (-1, 1), (1, -1), (1, 1))
TAPS = [(a, b) for a in range(3) for b in range(3)]


SIDE_COLS = (-3, -2, -1, 0)
PITCH = 9


class Tiles:
    def __init__(self, channels, rows, cols):
        self.channels, self.rows, self.cols = channels, rows, cols
        self.tall = rows + 2 * RIM
        self.total = (self.tall + 1) * LANES
        self.half = -(-9 * channels // (2 * LANES)) * LANES
        assert cols == LANES and self.tall * PITCH <= LANES
        groups = self.places()
        self.families = []
        for members in ((0,), (1,), (2, 3), (4, 5)):
            low = groups[members[0]][1]
            width = sum(len(groups[j][2]) for j in members)
            assert 4 * width <= LANES
            self.families.append((members, low, width))

    def side(self, row, col):
        return (row + RIM) * PITCH + (col + RIM if col <= 0 else col - self.cols + 6)

    def places(self):
        groups = []
        lane = 0
        for down, right in SIDES:
            rows = {0: range(self.rows), -1: range(self.rows - RIM, self.rows), 1: range(RIM)}[down]
            cols = {-1: range(self.cols - RIM, self.cols), 1: range(RIM)}[right]
            pairs = [(r, c) for r in rows for c in cols]
            groups.append(((down, right), lane, pairs))
            lane += len(pairs)
        assert lane <= LANES
        return groups

    def tables(self):
        kind = ml_dtypes.bfloat16
        pack = np.zeros((self.rows * LANES, LANES), kind)
        settle = np.zeros((LANES, LANES), kind)
        for (down, right), lane, pairs in self.places():
            for k, (r, c) in enumerate(pairs):
                pack[r * LANES + c, lane + k] = 1
                settle[lane + k, self.side(r + down * self.rows, c + right * self.cols)] = 1
        place = np.zeros((4, LANES, 4 * LANES), kind)
        unplace = np.zeros((4 * LANES, 4 * LANES), kind)
        for f, (_, low, width) in enumerate(self.families):
            for p in range(4):
                for i in range(width):
                    spot = f * LANES + p * width + i
                    place[p, low + i, spot] = 1
                    unplace[spot, p * LANES : (p + 1) * LANES] = settle[low + i]
        pick = np.zeros((self.tall * LANES, LANES), kind)
        where = np.zeros((8, self.total), np.int32)
        where[0, :] = -(10**6)
        for t in range(self.tall):
            where[0, t * LANES : (t + 1) * LANES] = t - RIM
            where[1, t * LANES : (t + 1) * LANES] = np.arange(LANES)
            for col in (0, self.cols - 2, self.cols - 1):
                pick[t * LANES + col, self.side(t - RIM, col)] = 1
            for col in SIDE_COLS + tuple(range(self.cols - 2, self.cols + RIM)):
                spot = self.tall * LANES + self.side(t - RIM, col)
                where[0, spot], where[1, spot] = t - RIM, col
        return pack, place, unplace, settle, pick, where


def dot(a, b):
    return jnp.dot(a, b, preferred_element_type=F32)


def dot_nt(a, b):
    return lax.dot_general(a, b, (((1,), (1,)), ((), ())), preferred_element_type=F32)


def dot_exact(values, table):
    high = values.astype(BF16)
    rest = values - high.astype(F32)
    middle = rest.astype(BF16)
    low = (rest - middle.astype(F32)).astype(BF16)
    return dot(high, table) + (dot(middle, table) + dot(low, table))


def rolled(values, shift):
    if shift % values.shape[1] == 0:
        return values
    return pltpu.roll(values, (-shift) % values.shape[1], axis=1)


def whole_kernel(tiles, row_count, col_count, *refs):
    sources = refs[:13]
    (perturb_rows, predict_rows, state, moment) = refs[13:17]
    held = refs[17:30]
    (image_in, perturb_in, target_in, pack, place, unplace, settle, pick, where) = held[:9]
    (k1_in, k2_in, m1_in, m2_in) = held[9:]
    (
        attacked, attacked_three, slope, hidden_three, rest, pre, pre_stack, pre_three,
        image, perturb, target_main, target, predicted,
        message, target_message, beside, target_beside,
        weights, back_wide, spread_wide, spread_weight,
        grad_wide, grad, grad_sent, grad_mate, plane, line, summed,
        load_sems, rim_sends, rim_recvs, sum_sends, sum_recvs, rows_wide, rows_short,
    ) = refs[30:]
    C, H, L, tall = tiles.channels, tiles.half, LANES, tiles.tall
    K, C3 = 9 * C, 3 * C
    rows, w = tiles.rows, tiles.cols
    own = slice(RIM * L, (RIM + rows) * L)
    me_row, me_col = lax.axis_index("rows"), lax.axis_index("cols")
    core, chip = lax.rem(me_row, 2), me_row // 2
    near, far = lax.rem(me_col, 2), me_col // 2
    chips, lines = row_count // 2, col_count // 2
    me_plane = chip * 2 + near
    last = REPLAYS - 1

    def exists(down, right):
        return (
            (me_row + down >= 0)
            & (me_row + down < row_count)
            & (me_col + right >= 0)
            & (me_col + right < col_count)
        )

    mate = {"rows": me_row + 1 - 2 * core, "cols": me_col}
    plane_peers = []
    for dx in range(chips):
        for dy in range(2):
            if dx or dy:
                there = lax.rem(chip + dx, chips) * 2 + core
                plane_peers.append({"rows": there, "cols": far * 2 + lax.rem(near + dy, 2)})
    line_peers = [
        {"rows": me_row, "cols": lax.rem(far + d, lines) * 2 + near} for d in range(1, lines)
    ]

    barrier = pltpu.get_barrier_semaphore()

    def signal(device):
        pl.semaphore_signal(barrier, inc=1, device_id=device, device_id_type=MESH)

    greeted = 1 + len(plane_peers) + len(line_peers)
    for device in line_peers + plane_peers + [mate]:
        signal(device)
    for down, right in SIDES + ((1, 0), (-1, 0)):
        there = exists(down, right)
        pl.when(there)(
            functools.partial(signal, {"rows": me_row + down, "cols": me_col + right})
        )
        greeted = greeted + there.astype(jnp.int32)

    loads = [
        pltpu.make_async_copy(source, target, load_sems.at[i])
        for i, (source, target) in enumerate(zip(sources, held))
    ]
    for load in loads:
        load.start()

    lane = lax.broadcasted_iota(jnp.int32, (1, L), 1)

    @pl.when(me_row == 0)
    def _():
        for k in range(REPLAYS):
            attacked[k, :, :, 0 : RIM * L] = jnp.zeros((4, C, RIM * L), BF16)
        target_main[0, :, 0 : RIM * L] = jnp.zeros((C, RIM * L), BF16)

    @pl.when(me_row == row_count - 1)
    def _():
        for k in range(REPLAYS):
            attacked[k, :, :, (RIM + rows) * L :] = jnp.zeros((4, C, RIM * L), BF16)
        target_main[0, :, (RIM + rows) * L :] = jnp.zeros((C, RIM * L), BF16)

    from_col = lax.broadcasted_iota(jnp.int32, (2 * w, 2 * w), 0)
    to_col = lax.broadcasted_iota(jnp.int32, (2 * w, 2 * w), 1)
    sorted_from = jnp.where(to_col < w, 2 * to_col, 2 * (to_col - w) + 1)
    order = (from_col == sorted_from).astype(F32).astype(BF16)
    high_rows = 2 * rows

    def spread_rows(parts, put):
        rows_wide[0] = parts[:, :w]
        rows_wide[1] = parts[:, w:]
        for r in range(rows):
            for py in range(2):
                for px in range(2):
                    part = rows_wide[px, pl.ds(2 * r + py, C, stride=high_rows), :]
                    put(2 * py + px, slice(r * L, (r + 1) * L), part)

    def put_image(p, spots, part):
        image[p, :, spots] = part.astype(BF16)

    def put_perturb(p, spots, part):
        perturb[p, :, spots] = part

    loads[0].wait()
    spread_rows(dot(image_in[...], order), put_image)
    loads[1].wait()
    spread_rows(dot_exact(perturb_in[...], order), put_perturb)
    for p in range(4):
        attacked[0, p, :, own] = (image[p].astype(F32) + perturb[p]).astype(BF16)
    loads[2].wait()
    rows_short[...] = target_in[...].astype(F32)
    for r in range(rows):
        spot = (RIM + r) * L
        target_main[0, :, spot : spot + L] = rows_short[pl.ds(r, C, stride=rows), :].astype(BF16)

    def make_message(k):
        phases = [dot(attacked[k, p, :, own], pack[...]).astype(BF16) for p in range(4)]
        total = dot(phases[0], place[0])
        for p in range(1, 4):
            total = total + dot(phases[p], place[p])
        for f in range(4):
            message[k, f] = total[:, f * L : (f + 1) * L].astype(BF16)

    loads[3].wait()
    loads[4].wait()
    make_message(0)
    target_message[...] = dot(target_main[0, :, own], pack[...]).astype(BF16)
    pl.semaphore_wait(barrier, greeted)

    def copy_of(source, target, sends, recvs, device):
        return pltpu.make_async_remote_copy(
            src_ref=source,
            dst_ref=target,
            send_sem=sends,
            recv_sem=recvs,
            device_id=device,
            device_id_type=MESH,
        )

    family_of = {j: f for f, (members, _, _) in enumerate(tiles.families) for j in members}

    def rim_copies(block, sides, to_beside, k):
        copies = []

        def add(source, target, down, right):
            i = len(copies)
            device = {"rows": me_row + down, "cols": me_col + right}
            copy = copy_of(source, target, rim_sends.at[k, i], rim_recvs.at[k, i], device)
            copies.append((copy, exists(down, right), exists(-down, -right)))

        for j, (down, right) in enumerate(SIDES):
            add(sides(j), to_beside.at[j], -down, -right)
        deep = RIM * L
        add(block.at[:, :, pl.ds(rows * L, deep)], block.at[:, :, pl.ds(0, deep)], 1, 0)
        add(block.at[:, :, pl.ds(deep, deep)], block.at[:, :, pl.ds(deep + rows * L, deep)], -1, 0)
        return copies

    def start(copies):
        for copy, there, _ in copies:
            pl.when(there)(copy.start)

    def finish(copies):
        for copy, there, here in copies:
            pl.when(there)(copy.wait_send)
            pl.when(here)(copy.wait_recv)

    def rim_of(k):
        return rim_copies(attacked.at[k], lambda j: message.at[k, family_of[j]], beside.at[k], k)

    begin = rim_of(0)
    start(begin)
    extra = rim_copies(target_main, lambda j: target_message, target_beside, REPLAYS)
    start(extra)

    for load in loads[5:]:
        load.wait()
    far_row, far_col = where[0:1, :] + me_row * rows, where[1:2, :] + me_col * w
    inside = (
        (far_row >= 0)
        & (far_row < rows * row_count)
        & (far_col >= 0)
        & (far_col < w * col_count)
    ).astype(F32)
    inside_side = inside[:, tall * L :]
    tall_one, tall_two, tall_three = rows + 4, rows + 3, rows + 2
    inside_one = jnp.concatenate([inside[:, L : (1 + tall_one) * L], inside_side], axis=1)
    inside_two = jnp.concatenate([inside[:, 2 * L : (2 + tall_two) * L], inside_side], axis=1)

    state[...] = jnp.zeros(state.shape, F32)
    moment[...] = jnp.zeros(moment.shape, F32)
    grad_wide[...] = jnp.zeros(grad_wide.shape, F32)
    weights[...] = jnp.zeros(weights.shape, F32)
    spread_wide[...] = jnp.zeros(spread_wide.shape, F32)
    pre_stack[...] = jnp.zeros(pre_stack.shape, BF16)
    for i in range(9):
        one, two = i * C, (i + 1) * C
        state[0, :, one:two] = k1_in[one:two, :]
        state[1, :, one:two] = k2_in[one:two, :]
        moment[0, :, one:two] = m1_in[one:two, :]
        moment[1, :, one:two] = m2_in[one:two, :]

    groups = tiles.places()
    slot_of = lax.rem(lane, PITCH)

    def turned(g):
        weights[0:C, :] = state[g]
        return jnp.transpose(weights[...])

    def spread_ready():
        wide = turned(1)
        for i, (a, b) in enumerate(TAPS):
            py, dy = [(1, 1), (0, 0), (1, 0)][a]
            px, dx = [(1, 1), (0, 0), (1, 0)][b]
            p, slot = 2 * py + px, 2 * dy + dx
            block = wide[i * C : (i + 1) * C, 0:C]
            spread_wide[p * C : (p + 1) * C, slot * C : (slot + 1) * C] = block
        spread_weight[...] = spread_wide[:, 0 : 4 * C].astype(BF16)

    def back_ready():
        wide = turned(0)
        for i, (a, b) in enumerate(TAPS):
            block = wide[i * C : (i + 1) * C, 0:C]
            back_wide[a * C : (a + 1) * C, b * C : (b + 1) * C] = block
        return back_wide[:, 0:C3].astype(BF16)

    def shifted(block, edge, by):
        end = 0 if by < 0 else L - 1
        return jnp.where(lane == end, edge, pltpu.roll(block, (-by) % L, axis=1))

    def edges(side):
        return jnp.where(slot_of == 2, side, pltpu.roll(side, L - 5, axis=1))

    def edge(both, row):
        return pltpu.roll(both, (-tiles.side(row, -1)) % L, axis=1)

    def attacked_ready(k):
        parts = []
        for members, _, width in tiles.families:
            part = jnp.zeros((C, L), F32)
            each = width // len(members)
            for m, j in enumerate(members):
                (down, right), _, _ = groups[j]
                inner = lax.rem(lane, width)
                keep = (inner >= m * each) & (inner < (m + 1) * each) & exists(down, right)
                part = jnp.where(keep, beside[k, j].astype(F32), part)
            parts.append(jnp.where(lane < 4 * width, part, 0.0).astype(BF16))
        around = dot(jnp.concatenate(parts, axis=1), unplace[...])
        for p in range(4):
            side = around[:, p * L : (p + 1) * L] + dot(attacked[k, p], pick[...])
            both = edges(side)
            for t in range(tall):
                spots = slice(t * L, (t + 1) * L)
                block = attacked[k, p, :, spots].astype(F32)
                ends = edge(both, t - RIM)
                attacked_three[p, 0:C, spots] = shifted(block, ends, -1).astype(BF16)
                attacked_three[p, C : 2 * C, spots] = attacked[k, p, :, spots]
                attacked_three[p, 2 * C :, spots] = shifted(block, ends, 1).astype(BF16)
            spots = slice(tall * L, (tall + 1) * L)
            attacked_three[p, 0:C, spots] = pltpu.roll(side, 1, axis=1).astype(BF16)
            attacked_three[p, C : 2 * C, spots] = side.astype(BF16)
            attacked_three[p, 2 * C :, spots] = pltpu.roll(side, L - 1, axis=1).astype(BF16)

    spread_ready()
    finish(begin)
    attacked_ready(0)
    finish(extra)
    gathered = jnp.zeros((C, L), F32)
    for j, ((down, right), first, pairs) in enumerate(groups):
        keep = (lane >= first) & (lane < first + len(pairs)) & exists(down, right)
        gathered = jnp.where(keep, target_beside[j].astype(F32), gathered)
    target[:, 0 : tall_two * L] = target_main[0, :, 2 * L : (2 + tall_two) * L].astype(F32)
    target[:, tall_two * L :] = dot(gathered.astype(BF16), settle[...]) + dot(
        target_main[0], pick[...]
    )

    def mate_copy(k, g):
        return copy_of(
            grad_sent.at[k, g, 1 - core],
            grad_mate.at[k, g],
            sum_sends.at[k, g, 0],
            sum_recvs.at[k, g, 0],
            mate,
        )

    def peer_copies(ref, index, peers, k, g, at):
        return [
            copy_of(
                ref.at[k, g, index],
                ref.at[k, g, index],
                sum_sends.at[k, g, at + i],
                sum_recvs.at[k, g, at + i],
                device,
            )
            for i, device in enumerate(peers)
        ]

    def plane_copies(k, g):
        return peer_copies(plane, me_plane, plane_peers, k, g, 2)

    def line_copies(k, g):
        return peer_copies(line, far, line_peers, k, g, 2 + len(plane_peers))

    def back_copies(k, g):
        return peer_copies(summed, core, [mate], k, g, 1)

    def begin_sum(k, g, parts):
        for a in range(3):
            grad_wide[g, :, a * C3 : (a + 1) * C3] = parts[a]
        for h in range(2):
            grad[g, h] = grad_wide[g, :, h * H : (h + 1) * H]
            grad_sent[k, g, h] = grad_wide[g, :, h * H : (h + 1) * H].astype(BF16)
        mate_copy(k, g).start()

    def plane_sum(k, g):
        mate_copy(k, g).wait()
        plane[k, g, me_plane] = (grad[g, core] + grad_mate[k, g].astype(F32)).astype(BF16)
        for copy in plane_copies(k, g):
            copy.start()

    def sum_of(ref, k, g, count):
        total = ref[k, g, 0].astype(F32)
        for i in range(1, count):
            total = total + ref[k, g, i].astype(F32)
        return total.astype(BF16)

    def line_sum(k, g):
        for copy in plane_copies(k, g):
            copy.wait()
        line[k, g, far] = sum_of(plane, k, g, 2 * chips)
        for copy in line_copies(k, g):
            copy.start()

    def back_sum(k, g):
        for copy in line_copies(k, g):
            copy.wait()
        summed[k, g, core] = sum_of(line, k, g, lines)
        for copy in back_copies(k, g):
            copy.start()

    def end_sum(k, g):
        for copy in back_copies(k, g):
            copy.wait()
        parts = [summed[k, g, h].astype(F32) for h in range(2)]
        squares = parts[0] * parts[0] + parts[1] * parts[1]
        mean = jnp.sum(jnp.sum(squares, axis=0, keepdims=True), axis=1, keepdims=True) / (K * C)
        unit = 1.0 / jnp.sqrt(mean + mean_epsilon)
        for h in range(2):
            later = momentum_rate * moment[g, :, h * H : (h + 1) * H] + parts[h] * unit
            moment[g, :, h * H : (h + 1) * H] = later
            state[g, :, h * H : (h + 1) * H] -= learn_rate * later

    def replay(k):
        fast_one = [state[0, :, a * C3 : (a + 1) * C3].astype(BF16) for a in range(3)]
        fast_two = [state[1, :, a * C3 : (a + 1) * C3].astype(BF16) for a in range(3)]
        ahead_one = jnp.concatenate(fast_one, axis=0)
        for p in (1, 3, 0, 2):
            sums = dot(ahead_one, attacked_three[p])
            main = (
                sums[0:C, 0 : tall_one * L]
                + sums[C : 2 * C, L : (1 + tall_one) * L]
                + sums[2 * C :, 2 * L : (2 + tall_one) * L]
            )
            side = sums[:, tall * L :]
            side = (
                pltpu.roll(side[0:C], PITCH, axis=1)
                + side[C : 2 * C]
                + pltpu.roll(side[2 * C :], L - PITCH, axis=1)
            )
            pre_value = jnp.concatenate([main, side], axis=1)
            sigmoid_value = jax.nn.sigmoid(pre_value)
            value = pre_value * sigmoid_value * inside_one
            slope_value = sigmoid_value * (1.0 + pre_value * (1.0 - sigmoid_value)) * inside_one
            slope[p, :, 0 : tall_three * L] = slope_value[:, L : (1 + tall_three) * L]
            slope[p, :, tall_three * L :] = slope_value[:, tall_one * L :]
            py, px = p // 2, p % 2
            if px == 0:
                hidden_three[py, C : 2 * C, :] = value.astype(BF16)
            else:
                hidden_three[py, 2 * C :, :] = value.astype(BF16)
                side = value[:, tall_one * L :]
                for t in range(tall_one):
                    spots = slice(t * L, (t + 1) * L)
                    moved = shifted(value[:, spots], edge(side, t - 2), -1)
                    hidden_three[py, 0:C, spots] = moved.astype(BF16)
                hidden_three[py, 0:C, tall_one * L :] = pltpu.roll(side, 1, axis=1).astype(BF16)

        outer = dot(jnp.concatenate([fast_two[0], fast_two[2]], axis=0), hidden_three[1])
        middle = dot(fast_two[1], hidden_three[0])
        main = (
            outer[0:C, 0 : tall_two * L]
            + outer[C:, L : (1 + tall_two) * L]
            + middle[:, L : (1 + tall_two) * L]
        )
        side = (
            pltpu.roll(outer[0:C, tall_one * L :], PITCH, axis=1)
            + outer[C:, tall_one * L :]
            + middle[:, tall_one * L :]
        )
        predicted[...] = main[:, L : (1 + rows) * L]
        predict = jnp.concatenate([main, side], axis=1)
        residual = ((predict - target[...]) * inside_two).astype(BF16)
        mine = residual[:, L : (1 + rows) * L]
        begin_sum(
            k,
            1,
            [
                dot_nt(mine, hidden_three[1, :, L : (1 + rows) * L]),
                dot_nt(mine, hidden_three[0, :, 2 * L : (2 + rows) * L]),
                dot_nt(mine, hidden_three[1, :, 2 * L : (2 + rows) * L]),
            ],
        )

        wide = residual.astype(F32)
        side = wide[:, tall_two * L :]
        for t in range(tall_two):
            spot = tiles.side(t - 1, 0)
            first = pltpu.roll(wide[:, t * L : (t + 1) * L], spot, axis=1)
            side = jnp.where(lane == spot, first, side)
        moved = []
        for t in range(tall_two):
            ends = pltpu.roll(side, (L - 1 - tiles.side(t - 1, w)) % L, axis=1)
            moved.append(shifted(wide[:, t * L : (t + 1) * L], ends, 1))
        moved = jnp.concatenate(moved, axis=1)
        moved_side = pltpu.roll(side, L - 1, axis=1)
        for i, (dy, block, beyond) in enumerate(
            ((0, wide, side), (0, moved, moved_side), (1, wide, side), (1, moved, moved_side))
        ):
            part = slice(i * C, (i + 1) * C)
            rest[part, 0 : tall_three * L] = block[:, dy * L : (dy + tall_three) * L].astype(BF16)
            beyond = rolled(beyond, dy * PITCH)
            rest[part, tall_three * L :] = beyond.astype(BF16)
        hidden_grad = dot(spread_weight[...], rest[...])
        total = jnp.zeros((C3, C3), F32)
        for p in range(4):
            if p == 3:
                plane_sum(k, 1)
            pre_grad = (hidden_grad[p * C : (p + 1) * C, :] * slope[p]).astype(BF16)
            pre[p] = pre_grad
            for a in range(3):
                part = slice(a * C, (a + 1) * C)
                pre_stack[p, part, a * L : (a + rows) * L] = pre_grad[:, L : (1 + rows) * L]
            total = total + dot_nt(pre_stack[p], attacked_three[p, :, 2 * L : (2 + tall_three) * L])
        begin_sum(k, 0, [total[a * C : (a + 1) * C, :] for a in range(3)])

        back_one = back_ready()

        def input_side(p):
            side = pre[p, :, tall_three * L :].astype(F32)
            both = edges(side)
            for t in range(tall_three):
                spots = slice(t * L, (t + 1) * L)
                block = pre[p, :, spots].astype(F32)
                ends = edge(both, t - 1)
                pre_three[0:C, spots] = shifted(block, ends, 1).astype(BF16)
                pre_three[C : 2 * C, spots] = pre[p, :, spots]
                pre_three[2 * C :, spots] = shifted(block, ends, -1).astype(BF16)
            sums = dot(back_one, pre_three[...])
            input_grad = (
                sums[0:C, 2 * L : (2 + rows) * L]
                + sums[C : 2 * C, L : (1 + rows) * L]
                + sums[2 * C :, 0 : rows * L]
            )
            moved = jnp.clip(perturb[p] + step_size * jnp.tanh(input_grad), -clip_bound, clip_bound)
            perturb[p] = moved
            attacked[k + 1, p, :, own] = (image[p].astype(F32) + moved).astype(BF16)

        input_side(0)
        input_side(1)
        plane_sum(k, 0)
        for p in range(2, 4):
            input_side(p)
        following = rim_of(k + 1)

        @pl.when(k < last)
        def _():
            make_message(k + 1)
            start(following)

        line_sum(k, 1)
        line_sum(k, 0)

        @pl.when(k < last)
        def _():
            finish(following)
            attacked_ready(k + 1)

        @pl.when(k == last)
        def _():
            for r in range(rows):
                spots = slice(r * L, (r + 1) * L)
                rows_short[pl.ds(r, C, stride=rows), :] = predicted[:, spots]
                for py in range(2):
                    for px in range(2):
                        part = perturb[2 * py + px, :, spots]
                        rows_wide[px, pl.ds(2 * r + py, C, stride=high_rows), :] = part
            predict_rows[...] = rows_short[...].astype(BF16)
            back_order = (
                lax.broadcasted_iota(jnp.int32, (2 * w, 2 * w), 1)
                == jnp.where(from_col < w, 2 * from_col, 2 * (from_col - w) + 1)
            ).astype(F32).astype(BF16)
            perturb_rows[...] = dot_exact(rows_wide[0], back_order[:w, :]) + dot_exact(
                rows_wide[1], back_order[w:, :]
            )

        for g in (1, 0):
            back_sum(k, g)
        end_sum(k, 1)
        spread_ready()
        end_sum(k, 0)

    @pl.loop(0, REPLAYS)
    def _(k):
        replay(k)


def finish_kernel(channels, *refs):
    perturb_in, predict_in, state, moment = refs[:4]
    outs, held, sems = refs[4:10], refs[10:14], refs[14]
    sources = [perturb_in, predict_in, *held]
    copies = [pltpu.make_async_copy(x, y, sems.at[i]) for i, (x, y) in enumerate(zip(sources, outs))]
    copies[0].start()
    copies[1].start()
    for n, (array, g) in enumerate(((state, 0), (state, 1), (moment, 0), (moment, 1))):
        for i in range(9):
            one, two = i * channels, (i + 1) * channels
            held[n][one:two, :] = array[g, :, one:two]
        copies[2 + n].start()
    for copy in copies:
        copy.wait()


def finished(channels, results):
    perturb, predict = results[:2]
    kernel = (9 * channels, channels)
    shapes = [jax.ShapeDtypeStruct(x.shape, x.dtype) for x in (perturb, predict)]
    shapes += [jax.ShapeDtypeStruct(kernel, F32)] * 4
    return pl.pallas_call(
        functools.partial(finish_kernel, channels),
        out_shape=shapes,
        in_specs=[WHOLE] * 4,
        out_specs=[pl.BlockSpec(memory_space=pl.ANY)] * 6,
        scratch_shapes=[pltpu.VMEM(kernel, F32)] * 4 + [pltpu.SemaphoreType.DMA((6,))],
        compiler_params=pltpu.CompilerParams(vmem_limit_bytes=FINISH_LIMIT),
    )(*results)


def whole(tiles, operands):
    C, H, L = tiles.channels, tiles.half, LANES
    K, C3, rows = 9 * C, 3 * C, tiles.rows
    row_count, col_count = lax.axis_size("rows"), lax.axis_size("cols")
    assert row_count % 2 == 0 and col_count % 2 == 0
    perturb, target = operands[1:3]
    shapes = [
        pltpu.VMEM(perturb.shape, F32),
        pltpu.VMEM(target.shape, BF16),
    ] + [pltpu.VMEM((2, C, 2 * H), F32)] * 2
    sums = 2 + (row_count - 1) + (col_count // 2 - 1)
    scratch = [pltpu.VMEM(x.shape, x.dtype) for x in operands] + [
        pltpu.VMEM((REPLAYS + 1, 4, C, tiles.tall * L), BF16),
        pltpu.VMEM((4, C3, tiles.total), BF16),
        pltpu.VMEM((4, C, (rows + 3) * L), F32),
        pltpu.VMEM((2, C3, (rows + 5) * L), BF16),
        pltpu.VMEM((4 * C, (rows + 3) * L), BF16),
        pltpu.VMEM((4, C, (rows + 3) * L), BF16),
        pltpu.VMEM((4, C3, (rows + 2) * L), BF16),
        pltpu.VMEM((C3, (rows + 2) * L), BF16),
        pltpu.VMEM((4, C, rows * L), BF16),
        pltpu.VMEM((4, C, rows * L), F32),
        pltpu.VMEM((1, C, tiles.tall * L), BF16),
        pltpu.VMEM((C, (rows + 4) * L), F32),
        pltpu.VMEM((C, rows * L), F32),
        pltpu.VMEM((REPLAYS, 4, C, L), BF16),
        pltpu.VMEM((C, L), BF16),
        pltpu.VMEM((REPLAYS, len(SIDES), C, L), BF16),
        pltpu.VMEM((len(SIDES), C, L), BF16),
        pltpu.VMEM((L, 2 * H), F32),
        pltpu.VMEM((C3, 2 * L), F32),
        pltpu.VMEM((4 * C, 2 * L), F32),
        pltpu.VMEM((4 * C, 4 * C), BF16),
        pltpu.VMEM((2, C, 2 * H), F32),
        pltpu.VMEM((2, 2, C, H), F32),
        pltpu.VMEM((REPLAYS, 2, 2, C, H), BF16),
        pltpu.VMEM((REPLAYS, 2, C, H), BF16),
        pltpu.VMEM((REPLAYS, 2, row_count, C, H), BF16),
        pltpu.VMEM((REPLAYS, 2, col_count // 2, C, H), BF16),
        pltpu.VMEM((REPLAYS, 2, 2, C, H), BF16),
        pltpu.SemaphoreType.DMA((len(operands),)),
        pltpu.SemaphoreType.DMA((REPLAYS + 1, 8)),
        pltpu.SemaphoreType.DMA((REPLAYS + 1, 8)),
        pltpu.SemaphoreType.DMA((REPLAYS, 2, sums)),
        pltpu.SemaphoreType.DMA((REPLAYS, 2, sums)),
        pltpu.VMEM((2, perturb.shape[0], L), F32),
        pltpu.VMEM(target.shape, F32),
    ]
    return pl.pallas_call(
        functools.partial(whole_kernel, tiles, row_count, col_count),
        out_shape=shapes,
        in_specs=[pl.BlockSpec(memory_space=pltpu.HBM)] * len(operands),
        out_specs=[WHOLE] * len(shapes),
        scratch_shapes=scratch,
        compiler_params=pltpu.CompilerParams(
            collective_id=0, has_side_effects=True, vmem_limit_bytes=VMEM_LIMIT
        ),
    )(*operands)


def body(image, perturb, target, *kernels):
    C = image.shape[0]
    tiles = Tiles(C, target.shape[1], target.shape[2])
    tables = [jnp.asarray(t) for t in tiles.tables()]
    merged = [x.reshape(-1, x.shape[2]) for x in (image, perturb, target)]
    kernels = [x.transpose(2, 3, 0, 1).reshape(9 * C, C) for x in kernels]
    results = whole(tiles, merged + tables + kernels)
    new_perturb, prediction, *kernels = finished(C, results)
    kernels = [x.reshape(3, 3, C, C).transpose(2, 3, 0, 1) for x in kernels]
    return (new_perturb.reshape(perturb.shape), prediction.reshape(target.shape), *kernels)


def solution(mesh):
    block = P(None, "rows", "cols")
    in_specs = (block, block, block, P(), P(), P(), P())
    out_specs = (block, block, P(), P(), P(), P())
    return jax.shard_map(body, mesh=mesh, in_specs=in_specs, out_specs=out_specs, check_vma=False)
```

```python
import functools

import jax
import jax.numpy as jnp
import ml_dtypes
import numpy as np
from jax import lax
from jax.experimental import pallas as pl
from jax.experimental.pallas import tpu as pltpu
from jax.sharding import PartitionSpec as P

REPLAYS = 3

step_size = 0.5
clip_bound = 0.5
momentum_rate = 0.9
learn_rate = 0.005
mean_epsilon = 1e-06

MESH = pl.DeviceIdType.MESH
BF16 = jnp.bfloat16
F32 = jnp.float32
RIM = 3
LANES = 128
VMEM_LIMIT = 56 * 1024 * 1024
FINISH_LIMIT = 16 * 1024 * 1024
WHOLE = pl.BlockSpec(memory_space=pltpu.VMEM)

SIDES = ((0, -1), (0, 1), (-1, -1), (-1, 1), (1, -1), (1, 1))
TAPS = [(a, b) for a in range(3) for b in range(3)]


SIDE_COLS = (-3, -2, -1, 0)
PITCH = 9


class Tiles:
    def __init__(self, channels, rows, cols):
        self.channels, self.rows, self.cols = channels, rows, cols
        self.tall = rows + 2 * RIM
        self.total = (self.tall + 1) * LANES
        self.half = -(-9 * channels // (2 * LANES)) * LANES
        assert cols == LANES and self.tall * PITCH <= LANES
        groups = self.places()
        self.families = []
        for members in ((0,), (1,), (2, 3), (4, 5)):
            low = groups[members[0]][1]
            width = sum(len(groups[j][2]) for j in members)
            assert 4 * width <= LANES
            self.families.append((members, low, width))

    def side(self, row, col):
        return (row + RIM) * PITCH + (col + RIM if col <= 0 else col - self.cols + 6)

    def places(self):
        groups = []
        lane = 0
        for down, right in SIDES:
            rows = {0: range(self.rows), -1: range(self.rows - RIM, self.rows), 1: range(RIM)}[down]
            cols = {-1: range(self.cols - RIM, self.cols), 1: range(RIM)}[right]
            pairs = [(r, c) for r in rows for c in cols]
            groups.append(((down, right), lane, pairs))
            lane += len(pairs)
        assert lane <= LANES
        return groups

    def tables(self):
        kind = ml_dtypes.bfloat16
        pack = np.zeros((self.rows * LANES, LANES), kind)
        settle = np.zeros((LANES, LANES), kind)
        for (down, right), lane, pairs in self.places():
            for k, (r, c) in enumerate(pairs):
                pack[r * LANES + c, lane + k] = 1
                settle[lane + k, self.side(r + down * self.rows, c + right * self.cols)] = 1
        place = np.zeros((4, LANES, 4 * LANES), kind)
        unplace = np.zeros((4 * LANES, 4 * LANES), kind)
        for f, (_, low, width) in enumerate(self.families):
            for p in range(4):
                for i in range(width):
                    spot = f * LANES + p * width + i
                    place[p, low + i, spot] = 1
                    unplace[spot, p * LANES : (p + 1) * LANES] = settle[low + i]
        pick = np.zeros((self.tall * LANES, LANES), kind)
        where = np.zeros((8, self.total), np.int32)
        where[0, :] = -(10**6)
        for t in range(self.tall):
            where[0, t * LANES : (t + 1) * LANES] = t - RIM
            where[1, t * LANES : (t + 1) * LANES] = np.arange(LANES)
            for col in (0, self.cols - 2, self.cols - 1):
                pick[t * LANES + col, self.side(t - RIM, col)] = 1
            for col in SIDE_COLS + tuple(range(self.cols - 2, self.cols + RIM)):
                spot = self.tall * LANES + self.side(t - RIM, col)
                where[0, spot], where[1, spot] = t - RIM, col
        return pack, place, unplace, settle, pick, where


def dot(a, b):
    return jnp.dot(a, b, preferred_element_type=F32)


def dot_nt(a, b):
    return lax.dot_general(a, b, (((1,), (1,)), ((), ())), preferred_element_type=F32)


def dot_exact(values, table):
    high = values.astype(BF16)
    rest = values - high.astype(F32)
    middle = rest.astype(BF16)
    low = (rest - middle.astype(F32)).astype(BF16)
    return dot(high, table) + (dot(middle, table) + dot(low, table))


def rolled(values, shift):
    if shift % values.shape[1] == 0:
        return values
    return pltpu.roll(values, (-shift) % values.shape[1], axis=1)


def whole_kernel(tiles, row_count, col_count, *refs):
    sources = refs[:13]
    (perturb_rows, predict_rows, state, moment) = refs[13:17]
    held = refs[17:30]
    (image_in, perturb_in, target_in, pack, place, unplace, settle, pick, where) = held[:9]
    (k1_in, k2_in, m1_in, m2_in) = held[9:]
    (
        attacked, attacked_three, slope, hidden_three, rest, pre, pre_stack, pre_three,
        image, perturb, target_main, target, predicted,
        message, target_message, beside, target_beside,
        weights, back_wide, spread_wide, spread_weight,
        grad_wide, grad, grad_sent, grad_mate, plane, line, summed,
        load_sems, rim_sends, rim_recvs, sum_sends, sum_recvs, rows_wide, rows_short,
    ) = refs[30:]
    C, H, L, tall = tiles.channels, tiles.half, LANES, tiles.tall
    K, C3 = 9 * C, 3 * C
    rows, w = tiles.rows, tiles.cols
    own = slice(RIM * L, (RIM + rows) * L)
    me_row, me_col = lax.axis_index("rows"), lax.axis_index("cols")
    core, chip = lax.rem(me_row, 2), me_row // 2
    near, far = lax.rem(me_col, 2), me_col // 2
    chips, lines = row_count // 2, col_count // 2
    me_plane = chip * 2 + near
    last = REPLAYS - 1

    def exists(down, right):
        return (
            (me_row + down >= 0)
            & (me_row + down < row_count)
            & (me_col + right >= 0)
            & (me_col + right < col_count)
        )

    mate = {"rows": me_row + 1 - 2 * core, "cols": me_col}
    plane_peers = []
    for dx in range(chips):
        for dy in range(2):
            if dx or dy:
                there = lax.rem(chip + dx, chips) * 2 + core
                plane_peers.append({"rows": there, "cols": far * 2 + lax.rem(near + dy, 2)})
    line_peers = [
        {"rows": me_row, "cols": lax.rem(far + d, lines) * 2 + near} for d in range(1, lines)
    ]

    barrier = pltpu.get_barrier_semaphore()

    def signal(device):
        pl.semaphore_signal(barrier, inc=1, device_id=device, device_id_type=MESH)

    greeted = 1 + len(plane_peers) + len(line_peers)
    for device in line_peers + plane_peers + [mate]:
        signal(device)
    for down, right in SIDES + ((1, 0), (-1, 0)):
        there = exists(down, right)
        pl.when(there)(
            functools.partial(signal, {"rows": me_row + down, "cols": me_col + right})
        )
        greeted = greeted + there.astype(jnp.int32)

    loads = [
        pltpu.make_async_copy(source, target, load_sems.at[i])
        for i, (source, target) in enumerate(zip(sources, held))
    ]
    for load in loads:
        load.start()

    lane = lax.broadcasted_iota(jnp.int32, (1, L), 1)

    @pl.when(me_row == 0)
    def _():
        for k in range(REPLAYS):
            attacked[k, :, :, 0 : RIM * L] = jnp.zeros((4, C, RIM * L), BF16)
        target_main[0, :, 0 : RIM * L] = jnp.zeros((C, RIM * L), BF16)

    @pl.when(me_row == row_count - 1)
    def _():
        for k in range(REPLAYS):
            attacked[k, :, :, (RIM + rows) * L :] = jnp.zeros((4, C, RIM * L), BF16)
        target_main[0, :, (RIM + rows) * L :] = jnp.zeros((C, RIM * L), BF16)

    from_col = lax.broadcasted_iota(jnp.int32, (2 * w, 2 * w), 0)
    to_col = lax.broadcasted_iota(jnp.int32, (2 * w, 2 * w), 1)
    sorted_from = jnp.where(to_col < w, 2 * to_col, 2 * (to_col - w) + 1)
    order = (from_col == sorted_from).astype(F32).astype(BF16)
    high_rows = 2 * rows

    def spread_rows(parts, put):
        rows_wide[0] = parts[:, :w]
        rows_wide[1] = parts[:, w:]
        for r in range(rows):
            for py in range(2):
                for px in range(2):
                    part = rows_wide[px, pl.ds(2 * r + py, C, stride=high_rows), :]
                    put(2 * py + px, slice(r * L, (r + 1) * L), part)

    def put_image(p, spots, part):
        image[p, :, spots] = part.astype(BF16)

    def put_perturb(p, spots, part):
        perturb[p, :, spots] = part

    loads[0].wait()
    spread_rows(dot(image_in[...], order), put_image)
    loads[1].wait()
    spread_rows(dot_exact(perturb_in[...], order), put_perturb)
    for p in range(4):
        attacked[0, p, :, own] = (image[p].astype(F32) + perturb[p]).astype(BF16)
    loads[2].wait()
    rows_short[...] = target_in[...].astype(F32)
    for r in range(rows):
        spot = (RIM + r) * L
        target_main[0, :, spot : spot + L] = rows_short[pl.ds(r, C, stride=rows), :].astype(BF16)

    def make_message(k):
        phases = [dot(attacked[k, p, :, own], pack[...]).astype(BF16) for p in range(4)]
        total = dot(phases[0], place[0])
        for p in range(1, 4):
            total = total + dot(phases[p], place[p])
        for f in range(4):
            message[k, f] = total[:, f * L : (f + 1) * L].astype(BF16)

    loads[3].wait()
    loads[4].wait()
    make_message(0)
    target_message[...] = dot(target_main[0, :, own], pack[...]).astype(BF16)
    pl.semaphore_wait(barrier, greeted)

    def copy_of(source, target, sends, recvs, device):
        return pltpu.make_async_remote_copy(
            src_ref=source,
            dst_ref=target,
            send_sem=sends,
            recv_sem=recvs,
            device_id=device,
            device_id_type=MESH,
        )

    family_of = {j: f for f, (members, _, _) in enumerate(tiles.families) for j in members}

    def rim_copies(block, sides, to_beside, k):
        copies = []

        def add(source, target, down, right):
            i = len(copies)
            device = {"rows": me_row + down, "cols": me_col + right}
            copy = copy_of(source, target, rim_sends.at[k, i], rim_recvs.at[k, i], device)
            copies.append((copy, exists(down, right), exists(-down, -right)))

        for j, (down, right) in enumerate(SIDES):
            add(sides(j), to_beside.at[j], -down, -right)
        deep = RIM * L
        add(block.at[:, :, pl.ds(rows * L, deep)], block.at[:, :, pl.ds(0, deep)], 1, 0)
        add(block.at[:, :, pl.ds(deep, deep)], block.at[:, :, pl.ds(deep + rows * L, deep)], -1, 0)
        return copies

    def start(copies):
        for copy, there, _ in copies:
            pl.when(there)(copy.start)

    def finish(copies):
        for copy, there, here in copies:
            pl.when(there)(copy.wait_send)
            pl.when(here)(copy.wait_recv)

    def rim_of(k):
        return rim_copies(attacked.at[k], lambda j: message.at[k, family_of[j]], beside.at[k], k)

    begin = rim_of(0)
    start(begin)
    extra = rim_copies(target_main, lambda j: target_message, target_beside, REPLAYS)
    start(extra)

    for load in loads[5:]:
        load.wait()
    far_row, far_col = where[0:1, :] + me_row * rows, where[1:2, :] + me_col * w
    inside = (
        (far_row >= 0)
        & (far_row < rows * row_count)
        & (far_col >= 0)
        & (far_col < w * col_count)
    ).astype(F32)
    inside_side = inside[:, tall * L :]
    tall_one, tall_two, tall_three = rows + 4, rows + 3, rows + 2
    inside_one = jnp.concatenate([inside[:, L : (1 + tall_one) * L], inside_side], axis=1)
    inside_two = jnp.concatenate([inside[:, 2 * L : (2 + tall_two) * L], inside_side], axis=1)

    state[...] = jnp.zeros(state.shape, F32)
    moment[...] = jnp.zeros(moment.shape, F32)
    grad_wide[...] = jnp.zeros(grad_wide.shape, F32)
    weights[...] = jnp.zeros(weights.shape, F32)
    spread_wide[...] = jnp.zeros(spread_wide.shape, F32)
    pre_stack[...] = jnp.zeros(pre_stack.shape, BF16)
    for i in range(9):
        one, two = i * C, (i + 1) * C
        state[0, :, one:two] = k1_in[one:two, :]
        state[1, :, one:two] = k2_in[one:two, :]
        moment[0, :, one:two] = m1_in[one:two, :]
        moment[1, :, one:two] = m2_in[one:two, :]

    groups = tiles.places()
    slot_of = lax.rem(lane, PITCH)

    def turned(g):
        weights[0:C, :] = state[g]
        return jnp.transpose(weights[...])

    def spread_ready():
        wide = turned(1)
        for i, (a, b) in enumerate(TAPS):
            py, dy = [(1, 1), (0, 0), (1, 0)][a]
            px, dx = [(1, 1), (0, 0), (1, 0)][b]
            p, slot = 2 * py + px, 2 * dy + dx
            block = wide[i * C : (i + 1) * C, 0:C]
            spread_wide[p * C : (p + 1) * C, slot * C : (slot + 1) * C] = block
        spread_weight[...] = spread_wide[:, 0 : 4 * C].astype(BF16)

    def back_ready():
        wide = turned(0)
        for i, (a, b) in enumerate(TAPS):
            block = wide[i * C : (i + 1) * C, 0:C]
            back_wide[a * C : (a + 1) * C, b * C : (b + 1) * C] = block
        return back_wide[:, 0:C3].astype(BF16)

    def shifted(block, edge, by):
        end = 0 if by < 0 else L - 1
        return jnp.where(lane == end, edge, pltpu.roll(block, (-by) % L, axis=1))

    def edges(side):
        return jnp.where(slot_of == 2, side, pltpu.roll(side, L - 5, axis=1))

    def edge(both, row):
        return pltpu.roll(both, (-tiles.side(row, -1)) % L, axis=1)

    def attacked_ready(k):
        parts = []
        for members, _, width in tiles.families:
            part = jnp.zeros((C, L), F32)
            each = width // len(members)
            for m, j in enumerate(members):
                (down, right), _, _ = groups[j]
                inner = lax.rem(lane, width)
                keep = (inner >= m * each) & (inner < (m + 1) * each) & exists(down, right)
                part = jnp.where(keep, beside[k, j].astype(F32), part)
            parts.append(jnp.where(lane < 4 * width, part, 0.0).astype(BF16))
        around = dot(jnp.concatenate(parts, axis=1), unplace[...])
        for p in range(4):
            side = around[:, p * L : (p + 1) * L] + dot(attacked[k, p], pick[...])
            both = edges(side)
            for t in range(tall):
                spots = slice(t * L, (t + 1) * L)
                block = attacked[k, p, :, spots].astype(F32)
                ends = edge(both, t - RIM)
                attacked_three[p, 0:C, spots] = shifted(block, ends, -1).astype(BF16)
                attacked_three[p, C : 2 * C, spots] = attacked[k, p, :, spots]
                attacked_three[p, 2 * C :, spots] = shifted(block, ends, 1).astype(BF16)
            spots = slice(tall * L, (tall + 1) * L)
            attacked_three[p, 0:C, spots] = pltpu.roll(side, 1, axis=1).astype(BF16)
            attacked_three[p, C : 2 * C, spots] = side.astype(BF16)
            attacked_three[p, 2 * C :, spots] = pltpu.roll(side, L - 1, axis=1).astype(BF16)

    spread_ready()
    finish(begin)
    attacked_ready(0)
    finish(extra)
    gathered = jnp.zeros((C, L), F32)
    for j, ((down, right), first, pairs) in enumerate(groups):
        keep = (lane >= first) & (lane < first + len(pairs)) & exists(down, right)
        gathered = jnp.where(keep, target_beside[j].astype(F32), gathered)
    target[:, 0 : tall_two * L] = target_main[0, :, 2 * L : (2 + tall_two) * L].astype(F32)
    target[:, tall_two * L :] = dot(gathered.astype(BF16), settle[...]) + dot(
        target_main[0], pick[...]
    )

    def mate_copy(k, g):
        return copy_of(
            grad_sent.at[k, g, 1 - core],
            grad_mate.at[k, g],
            sum_sends.at[k, g, 0],
            sum_recvs.at[k, g, 0],
            mate,
        )

    def peer_copies(ref, index, peers, k, g, at):
        return [
            copy_of(
                ref.at[k, g, index],
                ref.at[k, g, index],
                sum_sends.at[k, g, at + i],
                sum_recvs.at[k, g, at + i],
                device,
            )
            for i, device in enumerate(peers)
        ]

    def plane_copies(k, g):
        return peer_copies(plane, me_plane, plane_peers, k, g, 2)

    def line_copies(k, g):
        return peer_copies(line, far, line_peers, k, g, 2 + len(plane_peers))

    def back_copies(k, g):
        return peer_copies(summed, core, [mate], k, g, 1)

    def begin_sum(k, g, parts):
        for a in range(3):
            grad_wide[g, :, a * C3 : (a + 1) * C3] = parts[a]
        for h in range(2):
            grad[g, h] = grad_wide[g, :, h * H : (h + 1) * H]
            grad_sent[k, g, h] = grad_wide[g, :, h * H : (h + 1) * H].astype(BF16)
        mate_copy(k, g).start()

    def plane_sum(k, g):
        mate_copy(k, g).wait()
        plane[k, g, me_plane] = (grad[g, core] + grad_mate[k, g].astype(F32)).astype(BF16)
        for copy in plane_copies(k, g):
            copy.start()

    def sum_of(ref, k, g, count):
        total = ref[k, g, 0].astype(F32)
        for i in range(1, count):
            total = total + ref[k, g, i].astype(F32)
        return total.astype(BF16)

    def line_sum(k, g):
        for copy in plane_copies(k, g):
            copy.wait()
        line[k, g, far] = sum_of(plane, k, g, 2 * chips)
        for copy in line_copies(k, g):
            copy.start()

    def back_sum(k, g):
        for copy in line_copies(k, g):
            copy.wait()
        summed[k, g, core] = sum_of(line, k, g, lines)
        for copy in back_copies(k, g):
            copy.start()

    def end_sum(k, g):
        for copy in back_copies(k, g):
            copy.wait()
        parts = [summed[k, g, h].astype(F32) for h in range(2)]
        squares = parts[0] * parts[0] + parts[1] * parts[1]
        mean = jnp.sum(jnp.sum(squares, axis=0, keepdims=True), axis=1, keepdims=True) / (K * C)
        unit = 1.0 / jnp.sqrt(mean + mean_epsilon)
        for h in range(2):
            later = momentum_rate * moment[g, :, h * H : (h + 1) * H] + parts[h] * unit
            moment[g, :, h * H : (h + 1) * H] = later
            state[g, :, h * H : (h + 1) * H] -= learn_rate * later

    def replay(k):
        fast_one = [state[0, :, a * C3 : (a + 1) * C3].astype(BF16) for a in range(3)]
        fast_two = [state[1, :, a * C3 : (a + 1) * C3].astype(BF16) for a in range(3)]
        ahead_one = jnp.concatenate(fast_one, axis=0)
        for p in (1, 3, 0, 2):
            sums = dot(ahead_one, attacked_three[p])
            main = (
                sums[0:C, 0 : tall_one * L]
                + sums[C : 2 * C, L : (1 + tall_one) * L]
                + sums[2 * C :, 2 * L : (2 + tall_one) * L]
            )
            side = sums[:, tall * L :]
            side = (
                pltpu.roll(side[0:C], PITCH, axis=1)
                + side[C : 2 * C]
                + pltpu.roll(side[2 * C :], L - PITCH, axis=1)
            )
            pre_value = jnp.concatenate([main, side], axis=1)
            sigmoid_value = jax.nn.sigmoid(pre_value)
            value = pre_value * sigmoid_value * inside_one
            slope_value = sigmoid_value * (1.0 + pre_value * (1.0 - sigmoid_value)) * inside_one
            slope[p, :, 0 : tall_three * L] = slope_value[:, L : (1 + tall_three) * L]
            slope[p, :, tall_three * L :] = slope_value[:, tall_one * L :]
            py, px = p // 2, p % 2
            if px == 0:
                hidden_three[py, C : 2 * C, :] = value.astype(BF16)
            else:
                hidden_three[py, 2 * C :, :] = value.astype(BF16)
                side = value[:, tall_one * L :]
                for t in range(tall_one):
                    spots = slice(t * L, (t + 1) * L)
                    moved = shifted(value[:, spots], edge(side, t - 2), -1)
                    hidden_three[py, 0:C, spots] = moved.astype(BF16)
                hidden_three[py, 0:C, tall_one * L :] = pltpu.roll(side, 1, axis=1).astype(BF16)

        outer = dot(jnp.concatenate([fast_two[0], fast_two[2]], axis=0), hidden_three[1])
        middle = dot(fast_two[1], hidden_three[0])
        main = (
            outer[0:C, 0 : tall_two * L]
            + outer[C:, L : (1 + tall_two) * L]
            + middle[:, L : (1 + tall_two) * L]
        )
        side = (
            pltpu.roll(outer[0:C, tall_one * L :], PITCH, axis=1)
            + outer[C:, tall_one * L :]
            + middle[:, tall_one * L :]
        )
        predicted[...] = main[:, L : (1 + rows) * L]
        predict = jnp.concatenate([main, side], axis=1)
        residual = ((predict - target[...]) * inside_two).astype(BF16)
        mine = residual[:, L : (1 + rows) * L]
        begin_sum(
            k,
            1,
            [
                dot_nt(mine, hidden_three[1, :, L : (1 + rows) * L]),
                dot_nt(mine, hidden_three[0, :, 2 * L : (2 + rows) * L]),
                dot_nt(mine, hidden_three[1, :, 2 * L : (2 + rows) * L]),
            ],
        )

        wide = residual.astype(F32)
        side = wide[:, tall_two * L :]
        for t in range(tall_two):
            spot = tiles.side(t - 1, 0)
            first = pltpu.roll(wide[:, t * L : (t + 1) * L], spot, axis=1)
            side = jnp.where(lane == spot, first, side)
        moved = []
        for t in range(tall_two):
            ends = pltpu.roll(side, (L - 1 - tiles.side(t - 1, w)) % L, axis=1)
            moved.append(shifted(wide[:, t * L : (t + 1) * L], ends, 1))
        moved = jnp.concatenate(moved, axis=1)
        moved_side = pltpu.roll(side, L - 1, axis=1)
        for i, (dy, block, beyond) in enumerate(
            ((0, wide, side), (0, moved, moved_side), (1, wide, side), (1, moved, moved_side))
        ):
            part = slice(i * C, (i + 1) * C)
            rest[part, 0 : tall_three * L] = block[:, dy * L : (dy + tall_three) * L].astype(BF16)
            beyond = rolled(beyond, dy * PITCH)
            rest[part, tall_three * L :] = beyond.astype(BF16)
        hidden_grad = dot(spread_weight[...], rest[...])
        total = jnp.zeros((C3, C3), F32)
        for p in range(4):
            if p == 2:
                plane_sum(k, 1)
            pre_grad = (hidden_grad[p * C : (p + 1) * C, :] * slope[p]).astype(BF16)
            pre[p] = pre_grad
            for a in range(3):
                part = slice(a * C, (a + 1) * C)
                pre_stack[p, part, a * L : (a + rows) * L] = pre_grad[:, L : (1 + rows) * L]
            total = total + dot_nt(pre_stack[p], attacked_three[p, :, 2 * L : (2 + tall_three) * L])
        begin_sum(k, 0, [total[a * C : (a + 1) * C, :] for a in range(3)])

        back_one = back_ready()

        def input_side(p):
            side = pre[p, :, tall_three * L :].astype(F32)
            both = edges(side)
            for t in range(tall_three):
                spots = slice(t * L, (t + 1) * L)
                block = pre[p, :, spots].astype(F32)
                ends = edge(both, t - 1)
                pre_three[0:C, spots] = shifted(block, ends, 1).astype(BF16)
                pre_three[C : 2 * C, spots] = pre[p, :, spots]
                pre_three[2 * C :, spots] = shifted(block, ends, -1).astype(BF16)
            sums = dot(back_one, pre_three[...])
            input_grad = (
                sums[0:C, 2 * L : (2 + rows) * L]
                + sums[C : 2 * C, L : (1 + rows) * L]
                + sums[2 * C :, 0 : rows * L]
            )
            moved = jnp.clip(perturb[p] + step_size * jnp.tanh(input_grad), -clip_bound, clip_bound)
            perturb[p] = moved
            attacked[k + 1, p, :, own] = (image[p].astype(F32) + moved).astype(BF16)

        input_side(0)
        input_side(1)
        plane_sum(k, 0)
        for p in range(2, 4):
            input_side(p)
        following = rim_of(k + 1)

        @pl.when(k < last)
        def _():
            make_message(k + 1)
            start(following)

        line_sum(k, 1)
        line_sum(k, 0)

        @pl.when(k < last)
        def _():
            finish(following)
            attacked_ready(k + 1)

        @pl.when(k == last)
        def _():
            for r in range(rows):
                spots = slice(r * L, (r + 1) * L)
                rows_short[pl.ds(r, C, stride=rows), :] = predicted[:, spots]
                for py in range(2):
                    for px in range(2):
                        part = perturb[2 * py + px, :, spots]
                        rows_wide[px, pl.ds(2 * r + py, C, stride=high_rows), :] = part
            predict_rows[...] = rows_short[...].astype(BF16)
            back_order = (
                lax.broadcasted_iota(jnp.int32, (2 * w, 2 * w), 1)
                == jnp.where(from_col < w, 2 * from_col, 2 * (from_col - w) + 1)
            ).astype(F32).astype(BF16)
            perturb_rows[...] = dot_exact(rows_wide[0], back_order[:w, :]) + dot_exact(
                rows_wide[1], back_order[w:, :]
            )

        for g in (1, 0):
            back_sum(k, g)
        end_sum(k, 1)
        spread_ready()
        end_sum(k, 0)

    @pl.loop(0, REPLAYS)
    def _(k):
        replay(k)


def finish_kernel(channels, *refs):
    perturb_in, predict_in, state, moment = refs[:4]
    outs, held, sems = refs[4:10], refs[10:14], refs[14]
    sources = [perturb_in, predict_in, *held]
    copies = [pltpu.make_async_copy(x, y, sems.at[i]) for i, (x, y) in enumerate(zip(sources, outs))]
    copies[0].start()
    copies[1].start()
    for n, (array, g) in enumerate(((state, 0), (state, 1), (moment, 0), (moment, 1))):
        for i in range(9):
            one, two = i * channels, (i + 1) * channels
            held[n][one:two, :] = array[g, :, one:two]
        copies[2 + n].start()
    for copy in copies:
        copy.wait()


def finished(channels, results):
    perturb, predict = results[:2]
    kernel = (9 * channels, channels)
    shapes = [jax.ShapeDtypeStruct(x.shape, x.dtype) for x in (perturb, predict)]
    shapes += [jax.ShapeDtypeStruct(kernel, F32)] * 4
    return pl.pallas_call(
        functools.partial(finish_kernel, channels),
        out_shape=shapes,
        in_specs=[WHOLE] * 4,
        out_specs=[pl.BlockSpec(memory_space=pl.ANY)] * 6,
        scratch_shapes=[pltpu.VMEM(kernel, F32)] * 4 + [pltpu.SemaphoreType.DMA((6,))],
        compiler_params=pltpu.CompilerParams(vmem_limit_bytes=FINISH_LIMIT),
    )(*results)


def whole(tiles, operands):
    C, H, L = tiles.channels, tiles.half, LANES
    K, C3, rows = 9 * C, 3 * C, tiles.rows
    row_count, col_count = lax.axis_size("rows"), lax.axis_size("cols")
    assert row_count % 2 == 0 and col_count % 2 == 0
    perturb, target = operands[1:3]
    shapes = [
        pltpu.VMEM(perturb.shape, F32),
        pltpu.VMEM(target.shape, BF16),
    ] + [pltpu.VMEM((2, C, 2 * H), F32)] * 2
    sums = 2 + (row_count - 1) + (col_count // 2 - 1)
    scratch = [pltpu.VMEM(x.shape, x.dtype) for x in operands] + [
        pltpu.VMEM((REPLAYS + 1, 4, C, tiles.tall * L), BF16),
        pltpu.VMEM((4, C3, tiles.total), BF16),
        pltpu.VMEM((4, C, (rows + 3) * L), F32),
        pltpu.VMEM((2, C3, (rows + 5) * L), BF16),
        pltpu.VMEM((4 * C, (rows + 3) * L), BF16),
        pltpu.VMEM((4, C, (rows + 3) * L), BF16),
        pltpu.VMEM((4, C3, (rows + 2) * L), BF16),
        pltpu.VMEM((C3, (rows + 2) * L), BF16),
        pltpu.VMEM((4, C, rows * L), BF16),
        pltpu.VMEM((4, C, rows * L), F32),
        pltpu.VMEM((1, C, tiles.tall * L), BF16),
        pltpu.VMEM((C, (rows + 4) * L), F32),
        pltpu.VMEM((C, rows * L), F32),
        pltpu.VMEM((REPLAYS, 4, C, L), BF16),
        pltpu.VMEM((C, L), BF16),
        pltpu.VMEM((REPLAYS, len(SIDES), C, L), BF16),
        pltpu.VMEM((len(SIDES), C, L), BF16),
        pltpu.VMEM((L, 2 * H), F32),
        pltpu.VMEM((C3, 2 * L), F32),
        pltpu.VMEM((4 * C, 2 * L), F32),
        pltpu.VMEM((4 * C, 4 * C), BF16),
        pltpu.VMEM((2, C, 2 * H), F32),
        pltpu.VMEM((2, 2, C, H), F32),
        pltpu.VMEM((REPLAYS, 2, 2, C, H), BF16),
        pltpu.VMEM((REPLAYS, 2, C, H), BF16),
        pltpu.VMEM((REPLAYS, 2, row_count, C, H), BF16),
        pltpu.VMEM((REPLAYS, 2, col_count // 2, C, H), BF16),
        pltpu.VMEM((REPLAYS, 2, 2, C, H), BF16),
        pltpu.SemaphoreType.DMA((len(operands),)),
        pltpu.SemaphoreType.DMA((REPLAYS + 1, 8)),
        pltpu.SemaphoreType.DMA((REPLAYS + 1, 8)),
        pltpu.SemaphoreType.DMA((REPLAYS, 2, sums)),
        pltpu.SemaphoreType.DMA((REPLAYS, 2, sums)),
        pltpu.VMEM((2, perturb.shape[0], L), F32),
        pltpu.VMEM(target.shape, F32),
    ]
    return pl.pallas_call(
        functools.partial(whole_kernel, tiles, row_count, col_count),
        out_shape=shapes,
        in_specs=[pl.BlockSpec(memory_space=pltpu.HBM)] * len(operands),
        out_specs=[WHOLE] * len(shapes),
        scratch_shapes=scratch,
        compiler_params=pltpu.CompilerParams(
            collective_id=0, has_side_effects=True, vmem_limit_bytes=VMEM_LIMIT
        ),
    )(*operands)


def body(image, perturb, target, *kernels):
    C = image.shape[0]
    tiles = Tiles(C, target.shape[1], target.shape[2])
    tables = [jnp.asarray(t) for t in tiles.tables()]
    merged = [x.reshape(-1, x.shape[2]) for x in (image, perturb, target)]
    kernels = [x.transpose(2, 3, 0, 1).reshape(9 * C, C) for x in kernels]
    results = whole(tiles, merged + tables + kernels)
    new_perturb, prediction, *kernels = finished(C, results)
    kernels = [x.reshape(3, 3, C, C).transpose(2, 3, 0, 1) for x in kernels]
    return (new_perturb.reshape(perturb.shape), prediction.reshape(target.shape), *kernels)


def solution(mesh):
    block = P(None, "rows", "cols")
    in_specs = (block, block, block, P(), P(), P(), P())
    out_specs = (block, block, P(), P(), P(), P())
    return jax.shard_map(body, mesh=mesh, in_specs=in_specs, out_specs=out_specs, check_vma=False)
```
